32 devices in a mesh: ha: 8 (over z, core), wa: 4 (over y, x).
Axes of the slice: x: 2, y: 2, z: 4, core: 2. Of those that a mesh axis runs over, the one named last changes fastest.
Arguments:
- inputs: bfloat16 [32, 256, 512], P('ha', 'wa'), may hold values from -6 to 6
- grad_out: bfloat16 [32, 256, 512], P('ha', 'wa'), may hold values from -6 to 6
- kernel_one: bfloat16 [27, 64, 64], replicated, may hold values from -0.15625 to 0.15625
- kernel_two: bfloat16 [27, 64, 64], replicated, may hold values from -0.15625 to 0.15625
Outputs:
- grad_inputs: bfloat16 [32, 256, 512], P('ha', 'wa')
- grad_kernel_one: float32 [110592], P(('ha', 'wa'))
- grad_kernel_two: float32 [110592], P(('ha', 'wa'))
The draws below stay inside these ranges and needn't reach their ends.
All inputs are finite; a program needn't handle non-finite values.
Results may differ from the reference program's by a relative error of at most 0.0049.
Values may be sent and summed in bfloat16 or wider, within the bound.
No kernel may reach another device: no remote copies, remote signals or barrier semaphores. Data moves between devices by JAX's collectives and lax.ppermute only.
A program may use at most 64 MiB of HBM per device.

```python
import jax
import jax.numpy as jnp
from jax import lax

CH = 64
DEPTH = 8
HEIGHT = 32
WIDTH = 256


def shard_levels(rng, extent, split, smallest, top_value):
    factor_of, own = 1.0, jax.random.fold_in(rng, 6)
    for dim, blocks in split:
        heights = jnp.exp(jax.random.uniform(jax.random.fold_in(own, dim), (blocks,), jnp.float32, smallest / len(split), top_value / len(split)))
        factor_of = factor_of * jnp.repeat(heights, extent[dim] // blocks).reshape([-1 if axis == dim else 1 for axis in range(len(extent))])
    return factor_of


def normal_values(stream_key, extent, deviation, bound, split=(), dtype=jnp.bfloat16):
    entries = jax.random.normal(stream_key, extent, jnp.float32) * deviation
    if len(split) > 0:
        entries = shard_levels(stream_key, extent, split, -0.22, 0.18) * entries
    return jnp.clip(entries, min=-bound, max=bound).astype(dtype)


def setup_inputs(seed: int = 0) -> dict:
    key_of = jax.random.split(jax.random.key(seed), 5)
    return {
        "inputs": normal_values(key_of[0], (HEIGHT, WIDTH, DEPTH * CH), 1.0, 6.0, ((0, 8), (1, 4))),
        "grad_out": normal_values(key_of[1], (HEIGHT, WIDTH, DEPTH * CH), 1.0, 6.0, ((0, 8), (1, 4))),
        "kernel_one": normal_values(key_of[2], (27, CH, CH), (27 * CH) ** -0.5, 0.15625),
        "kernel_two": normal_values(key_of[3], (27, CH, CH), (27 * CH) ** -0.5, 0.15625),
    }


root_half = 0.7071067811865476
inv_root_two_pi = 0.3989422804014327

def gelu_value(values):
    return 0.5 * values * (1.0 + jax.scipy.special.erf(values * root_half))

def gelu_slope(values):
    return 0.5 * (1.0 + jax.scipy.special.erf(values * root_half)) + values * inv_root_two_pi * jnp.exp(-0.5 * values * values)

def flip_kernel(kernel):
    return jnp.swapaxes(kernel[::-1], 1, 2)

def correlate(volume, kernel):
    left = volume.astype(jnp.float32)[None]
    right = kernel.astype(jnp.float32).reshape(3, 3, 3, kernel.shape[1], kernel.shape[2])
    result = lax.conv_general_dilated(left, right, (1, 1, 1), ((1, 1), (1, 1), (1, 1)), dimension_numbers=('NDHWC', 'DHWIO', 'NDHWC'), precision=lax.Precision.HIGHEST)
    return result[0]

def kernel_grad(source, cotangent):
    rows_here, cols_here, depth_cells, chans = cotangent.shape
    padded = jnp.pad(source, ((1, 1), (1, 1), (1, 1), (0, 0)))
    flat_cot = cotangent.astype(jnp.float32).reshape(-1, chans)
    pieces = []
    for position in range(27):
        rise_shift, side_shift, deep_shift = (position // 9, position // 3 % 3, position % 3)
        window = padded[rise_shift:rise_shift + rows_here, side_shift:side_shift + cols_here, deep_shift:deep_shift + depth_cells]
        window = window.astype(jnp.float32).reshape(-1, chans)
        pieces.append(jnp.dot(window.T, flat_cot, precision=lax.Precision.HIGHEST))
    return jnp.stack(pieces)

def reference(inputs, grad_out, kernel_one, kernel_two):
    volume = inputs.reshape(HEIGHT, WIDTH, DEPTH, CH)
    cotangent = grad_out.reshape(HEIGHT, WIDTH, DEPTH, CH)
    pre_active = correlate(volume, kernel_one)
    active = gelu_value(pre_active).astype(jnp.bfloat16)
    grad_active = correlate(cotangent, flip_kernel(kernel_two))
    grad_pre = (grad_active * gelu_slope(pre_active)).astype(jnp.bfloat16)
    grad_inputs = correlate(grad_pre, flip_kernel(kernel_one)).astype(jnp.bfloat16).reshape(HEIGHT, WIDTH, DEPTH * CH)
    grad_kernel_one = kernel_grad(volume, grad_pre).reshape(-1)
    grad_kernel_two = kernel_grad(active, cotangent).reshape(-1)
    return (grad_inputs, grad_kernel_one, grad_kernel_two)
```

```python
import functools

import jax
import jax.numpy as jnp
from jax import lax
from jax.experimental import pallas as pl
from jax.experimental.pallas import tpu as pltpu
from jax.sharding import PartitionSpec as P

CH = 64
PAD = 16

root_half = 0.7071067811865476
inv_root_two_pi = 0.3989422804014327


def pair_exchange(block, axis, first):
    count = lax.axis_size(axis)
    pairs = []
    for low in range(first, count - 1, 2):
        pairs += [(low, low + 1), (low + 1, low)]
    return lax.ppermute(block, axis, pairs)


def prepare_kernel(one_ref, two_ref, one_out, two_flip_out, one_flip_out):
    zero = jnp.zeros((CH, CH), jnp.bfloat16)

    def banded(tiles):
        padded = [zero] + tiles + [zero]
        return [jnp.concatenate([padded[c + 1], padded[c]], axis=1) for c in range(4)]

    def flipped(ref, tap):
        return jnp.transpose(ref[26 - tap].astype(jnp.float32)).astype(jnp.bfloat16)

    for ab in range(9):
        taps = [3 * ab + c for c in range(3)]
        for c, tile in enumerate(banded([one_ref[t] for t in taps])):
            one_out[ab, c] = tile
        for c, tile in enumerate(banded([flipped(two_ref, t) for t in taps])):
            two_flip_out[ab, c] = tile
        for c, tile in enumerate(banded([flipped(one_ref, t) for t in taps])):
            one_flip_out[ab, c] = tile


def prepare(kernel_one, kernel_two):
    shape = jax.ShapeDtypeStruct((9, 4, CH, 2 * CH), jnp.bfloat16)
    vmem = pl.BlockSpec(memory_space=pltpu.VMEM)
    return pl.pallas_call(
        prepare_kernel,
        out_shape=(shape, shape, shape),
        in_specs=[vmem, vmem],
        out_specs=(vmem, vmem, vmem),
        compiler_params=pltpu.CompilerParams(vmem_limit_bytes=16 << 20),
        cost_estimate=pl.CostEstimate(
            flops=4_000_000, bytes_accessed=4_000_000, transcendentals=0
        ),
    )(kernel_one, kernel_two)


def banded_weights(band_ref, group):
    zero = jnp.zeros((CH, 2 * CH), jnp.bfloat16)
    lift = 1 if group == 0 else -1
    rows = []
    for ab in range(9):
        for i in range(6):
            halves = []
            for m in range(2):
                c = i - 2 * m + lift
                halves.append(band_ref[ab, c] if 0 <= c < 4 else zero)
            rows.append(jnp.concatenate(halves, axis=1))
    return jnp.concatenate(rows, axis=0)


def main_kernel(
    rows,
    cols,
    x_ref,
    g_ref,
    ra_ref,
    rb_ref,
    ca_ref,
    cb_ref,
    one_ref,
    two_flip_ref,
    one_flip_ref,
    gi_ref,
    kg_ref,
    wide,
    xs,
    gs,
    ps,
    sums,
    acc_ref,
):
    f32, bf16 = jnp.float32, jnp.bfloat16
    stride = cols + PAD
    lines = rows + 4
    span = lines * stride + PAD
    lanes = x_ref.shape[2]
    base = 8
    ha = lax.axis_index("ha")
    wa = lax.axis_index("wa")
    ha_odd = lax.rem(ha, 2)
    wa_odd = lax.rem(wa, 2)

    halo = 2 * lines
    gap_rows = (lines + 1) * PAD
    q = lax.broadcasted_iota(jnp.int32, (gap_rows, 2 * halo), 0)
    col = lax.broadcasted_iota(jnp.int32, (gap_rows, 2 * halo), 1)
    gap = lax.div(q, PAD)
    w = lax.rem(q, PAD)

    def order(line):
        swapped = jnp.where(
            line < 2, line + lines - 2, jnp.where(line >= lines - 2, line - lines + 2, line)
        )
        return jnp.where(ha_odd == 0, swapped, line)

    left_base = jnp.where(wa_odd == 0, halo, 0)
    right_base = jnp.where(wa_odd == 0, 0, halo)
    left_hit = (w >= PAD - 2) & (gap < lines) & (col == left_base + 2 * order(gap) + w - (PAD - 2))
    right_hit = (w < 2) & (gap >= 1) & (col == right_base + 2 * order(gap - 1) + w)
    select = jnp.where(left_hit | right_hit, 1.0, 0.0).astype(bf16)

    def spread(which, own_ref, out):
        columns = jnp.concatenate([ca_ref[which], cb_ref[which]], axis=0)
        gaps = jnp.dot(select, columns, preferred_element_type=f32)
        for k in range(lines + 1):
            wide[base + k * stride : base + k * stride + PAD, :] = gaps[k * PAD : (k + 1) * PAD]
        for r in range(rows):
            start = base + PAD + (r + 2) * stride
            wide[start : start + cols, :] = own_ref[r].astype(f32)
        above = base + PAD
        below = base + PAD + (rows + 2) * stride
        a_start = jnp.where(ha_odd == 0, below, above)
        b_start = jnp.where(ha_odd == 0, above, below)
        for r in range(2):
            wide[pl.ds(pl.multiple_of(a_start + r * stride, 8), cols), :] = ra_ref[which, r].astype(f32)
            wide[pl.ds(pl.multiple_of(b_start + r * stride, 8), cols), :] = rb_ref[which, r].astype(f32)
        for b in range(3):
            out[b] = wide[base + b - 1 : base + b - 1 + span, :].astype(bf16)

    spread(0, x_ref, xs)
    spread(1, g_ref, gs)

    def correlate(src, band_ref, start, count):
        outs = []
        for group in range(2):
            lane = 128 * group
            left = jnp.concatenate(
                [
                    src[ab % 3, start + (ab // 3 - 1) * stride : start + (ab // 3 - 1) * stride + count, lane : lane + 6 * CH]
                    for ab in range(9)
                ],
                axis=1,
            )
            outs.append(jnp.dot(left, banded_weights(band_ref, group), preferred_element_type=f32))
        return outs

    first = stride
    count = (rows + 2) * stride + PAD
    pre = correlate(xs, one_ref, first, count)
    grad_active = correlate(gs, two_flip_ref, first, count)

    position = first + lax.broadcasted_iota(jnp.int32, (count, 256), 0)
    line = lax.div(position, stride)
    w = lax.rem(position, stride)
    ha_last = lax.axis_size("ha") - 1
    wa_last = lax.axis_size("wa") - 1
    owner = jnp.where(w < PAD // 2, line - 1, line)
    dead = ((owner < 2) & (ha == 0)) | ((owner >= rows + 2) & (ha == ha_last))
    dead = dead | ((w >= PAD // 2) & (w < PAD) & (wa == 0)) | ((w < PAD // 2) & (wa == wa_last))

    own_line = [PAD + (r + 1) * stride for r in range(rows)]
    active_t = []
    for group in range(2):
        value = pre[group]
        cdf = 0.5 * (1.0 + lax.erf(value * root_half))
        slope = cdf + value * inv_root_two_pi * jnp.exp(-0.5 * value * value)
        grad_pre = jnp.where(dead, 0.0, grad_active[group] * slope)
        wide[base + first : base + first + count, 256 * group : 256 * group + 256] = (
            grad_pre.astype(bf16).astype(f32)
        )
        active = value * cdf
        active = jnp.concatenate([active[s : s + cols] for s in own_line], axis=0)
        active_t.append(jnp.transpose(active).astype(bf16))
    for b in range(3):
        ps[b, first : first + count, :] = wide[
            base + first + b - 1 : base + first + b - 1 + count, :
        ].astype(bf16)

    x_own = jnp.concatenate([x_ref[r] for r in range(rows)], axis=0).astype(f32)
    x_t = [jnp.transpose(x_own[:, 256 * group : 256 * group + 256]).astype(bf16) for group in range(2)]

    def kernel_grad(fixed, src, a):
        parts = [[[None] * 4 for _ in range(3)] for _ in range(1)][0]
        for group in range(2):
            lane = 128 * group
            windows = []
            for b in range(3):
                shift = (1 - a) * stride
                windows.append(
                    jnp.concatenate(
                        [
                            src[2 - b, PAD + (r + 2) * stride + shift : PAD + (r + 2) * stride + shift + cols, lane : lane + 6 * CH]
                            for r in range(rows)
                        ],
                        axis=0,
                    )
                )
            acc_ref[...] = jnp.dot(
                fixed[group], jnp.concatenate(windows, axis=1), preferred_element_type=f32
            )
            lift = 1 if group == 0 else 3
            for b in range(3):
                for j in range(4):
                    for m in range(3):
                        e = j - 2 * m + lift
                        if 0 <= e < 4:
                            tile = acc_ref[64 * j : 64 * j + 64, 384 * b + 128 * m : 384 * b + 128 * m + 128]
                            old = parts[b][e]
                            parts[b][e] = tile if old is None else old + tile
        return parts

    low = lax.broadcasted_iota(jnp.int32, (CH, 2 * CH), 1) < CH
    for a in range(3):
        one = kernel_grad(x_t, ps, a)
        two = kernel_grad(active_t, gs, a)
        for b in range(3):
            for c in range(3):
                k_one = one[b][c] + pltpu.roll(one[b][c + 1], CH, 1)
                k_two = pltpu.roll(two[b][c], CH, 1) + two[b][c + 1]
                tap = 9 * a + 3 * b + c
                sums[CH * tap : CH * tap + CH, :] = jnp.where(low, k_one, k_two)
    share = kg_ref.shape[1]
    take = 27 * CH // kg_ref.shape[0]
    for d in range(kg_ref.shape[0]):
        kg_ref[d] = sums[take * d : take * d + share, :].astype(bf16)

    start = PAD + 2 * stride
    grad_inputs = correlate(ps, one_flip_ref, start, (rows - 1) * stride + cols)
    for group in range(2):
        for r in range(rows):
            gi_ref[r, :, 256 * group : 256 * group + 256] = grad_inputs[group][
                r * stride : r * stride + cols
            ].astype(bf16)


def main(x, g, ra, rb, ca, cb, one, two_flip, one_flip, devices):
    rows, cols, lanes = x.shape
    stride = cols + PAD
    span = (rows + 4) * stride + PAD
    take = 27 * CH // devices
    share = -(-take // 8) * 8
    vmem = pl.BlockSpec(memory_space=pltpu.VMEM)
    moving = pltpu.VMEM((3, span, lanes), jnp.bfloat16)
    return pl.pallas_call(
        functools.partial(main_kernel, rows, cols),
        out_shape=(
            jax.ShapeDtypeStruct(x.shape, jnp.bfloat16),
            jax.ShapeDtypeStruct((devices, share, 2 * CH), jnp.bfloat16),
        ),
        in_specs=[vmem] * 9,
        out_specs=(vmem, vmem),
        scratch_shapes=[
            pltpu.VMEM((span + 16, lanes), jnp.float32),
            moving,
            moving,
            moving,
            pltpu.VMEM((27 * CH + 8, 2 * CH), jnp.float32),
            pltpu.VMEM((256, 1152), jnp.float32),
        ],
        compiler_params=pltpu.CompilerParams(vmem_limit_bytes=48 << 20),
        cost_estimate=pl.CostEstimate(
            flops=20_000_000_000, bytes_accessed=8_000_000, transcendentals=1_000_000
        ),
    )(x, g, ra, rb, ca, cb, one, two_flip, one_flip)


def shards(inputs, grad_out, kernel_one, kernel_two):
    rows, cols, lanes = inputs.shape
    height_count = lax.axis_size("ha")
    width_count = lax.axis_size("wa")
    devices = height_count * width_count
    ha_even = lax.rem(lax.axis_index("ha"), 2) == 0
    wa_even = lax.rem(lax.axis_index("wa"), 2) == 0
    both = jnp.stack([inputs, grad_out])
    low, high = both[:, :2], both[:, rows - 2 :]
    ra = pair_exchange(jnp.where(ha_even, high, low), "ha", 0)
    rb = pair_exchange(jnp.where(ha_even, low, high), "ha", 1)
    one, two_flip, one_flip = prepare(kernel_one, kernel_two)

    def edge(start):
        pieces = [part[:, :, start : start + 2] for part in (ra, both, rb)]
        return jnp.concatenate(pieces, axis=1).reshape(2, 2 * (rows + 4), lanes)

    left, right = edge(0), edge(cols - 2)
    ca = pair_exchange(jnp.where(wa_even, right, left), "wa", 0)
    cb = pair_exchange(jnp.where(wa_even, left, right), "wa", 1)
    units = devices if (27 * CH) % devices == 0 else 1
    grad_inputs, partial = main(
        inputs, grad_out, ra, rb, ca, cb, one, two_flip, one_flip, units
    )
    if units == devices:
        take = 27 * CH // devices
        pieces = lax.all_to_all(partial, ("ha", "wa"), 0, 0, tiled=True)
        total = pieces.astype(jnp.float32).sum(0)[:take]
        return (
            grad_inputs,
            total[:, :CH].reshape(-1),
            total[:, CH:].reshape(-1),
        )
    partial = partial[0].astype(jnp.float32)
    outs = [partial[:, :CH].reshape(devices, -1), partial[:, CH:].reshape(devices, -1)]
    outs = [lax.psum_scatter(v, ("ha", "wa"), scatter_dimension=0, tiled=True) for v in outs]
    return (grad_inputs, outs[0].reshape(-1), outs[1].reshape(-1))


def solution(mesh):
    return jax.shard_map(
        shards,
        mesh=mesh,
        in_specs=(P("ha", "wa", None), P("ha", "wa", None), P(), P()),
        out_specs=(P("ha", "wa", None), P(("ha", "wa")), P(("ha", "wa"))),
        check_vma=False,
    )
```

```python
import functools

import jax
import jax.numpy as jnp
from jax import lax
from jax.experimental import pallas as pl
from jax.experimental.pallas import tpu as pltpu
from jax.sharding import PartitionSpec as P


CH = 64
PAD = 16

root_half = 0.7071067811865476
inv_root_two_pi = 0.3989422804014327


def pair_exchange(block, axis, first):
    count = lax.axis_size(axis)
    pairs = []
    for low in range(first, count - 1, 2):
        pairs += [(low, low + 1), (low + 1, low)]
    return lax.ppermute(block, axis, pairs)


def in_hbm(block):
    return pltpu.with_memory_space_constraint(block, pltpu.HBM)


def pack_kernel(x_hbm, g_hbm, x_ref, g_ref, to_a, to_b, own_a, own_b, sems):
    rows, cols, _ = x_ref.shape
    pairs = ((x_hbm, x_ref), (g_hbm, g_ref))
    copies = [
        pltpu.make_async_copy(source, target, sems.at[k])
        for k, (source, target) in enumerate(pairs)
    ]
    for copy in copies:
        copy.start()
    ha_even = lax.rem(lax.axis_index("ha"), 2) == 0
    wa_even = lax.rem(lax.axis_index("wa"), 2) == 0
    a_start = jnp.where(ha_even, rows - 2, 0)
    b_start = jnp.where(ha_even, 0, rows - 2)
    for which, ref in enumerate((x_ref, g_ref)):
        copies[which].wait()
        to_a[which] = ref[pl.ds(a_start, 2)]
        to_b[which] = ref[pl.ds(b_start, 2)]
        for r in range(rows):
            left, right = ref[r, 0:2, :], ref[r, cols - 2 : cols, :]
            own_a[which, r] = jnp.where(wa_even, right, left)
            own_b[which, r] = jnp.where(wa_even, left, right)


def pack(x, g):
    rows, cols, lanes = x.shape
    vmem = pl.BlockSpec(memory_space=pltpu.VMEM)
    hbm = pl.BlockSpec(memory_space=pltpu.HBM)
    shapes = [x.shape] * 2 + [(2, 2, cols, lanes)] * 2 + [(2, rows, 2, lanes)] * 2
    return pl.pallas_call(
        pack_kernel,
        out_shape=tuple(jax.ShapeDtypeStruct(shape, x.dtype) for shape in shapes),
        in_specs=[hbm, hbm],
        out_specs=(vmem,) * 6,
        scratch_shapes=[pltpu.SemaphoreType.DMA((2,))],
        compiler_params=pltpu.CompilerParams(vmem_limit_bytes=4 << 20),
        cost_estimate=pl.CostEstimate(flops=0, bytes_accessed=1_100_000, transcendentals=0),
    )(in_hbm(x), in_hbm(g))


def corners_kernel(wa_ref, wb_ref, to_a, to_b):
    rows = wa_ref.shape[1]
    ha_even = lax.rem(lax.axis_index("ha"), 2) == 0
    a_start = jnp.where(ha_even, rows - 2, 0)
    b_start = jnp.where(ha_even, 0, rows - 2)
    for side, ref in enumerate((wa_ref, wb_ref)):
        for which in range(2):
            for r in range(2):
                to_a[side, which, r] = ref[which, a_start + r]
                to_b[side, which, r] = ref[which, b_start + r]


def small_call(kernel, out_shape, *operands):
    vmem = pl.BlockSpec(memory_space=pltpu.VMEM)
    return pl.pallas_call(
        kernel,
        out_shape=out_shape,
        in_specs=[vmem] * len(operands),
        out_specs=(vmem,) * len(out_shape),
        compiler_params=pltpu.CompilerParams(vmem_limit_bytes=2 << 20),
        cost_estimate=pl.CostEstimate(flops=0, bytes_accessed=300_000, transcendentals=0),
    )(*operands)


def corners(wa, wb):
    shape = jax.ShapeDtypeStruct((2, 2, 2) + wa.shape[2:], wa.dtype)
    return small_call(corners_kernel, (shape, shape), wa, wb)


def prepare_kernel(
    one_hbm, two_hbm, one_out, two_flip_out, one_flip_out, one_ref, two_ref, sems
):
    copies = [
        pltpu.make_async_copy(one_hbm, one_ref, sems.at[0]),
        pltpu.make_async_copy(two_hbm, two_ref, sems.at[1]),
    ]
    for copy in copies:
        copy.start()
    for copy in copies:
        copy.wait()
    zero = jnp.zeros((CH, CH), jnp.bfloat16)

    def banded(tiles):
        padded = [zero] + tiles + [zero]
        return [jnp.concatenate([padded[c + 1], padded[c]], axis=1) for c in range(4)]

    def flipped(ref, tap):
        return jnp.transpose(ref[26 - tap].astype(jnp.float32)).astype(jnp.bfloat16)

    for ab in range(9):
        taps = [3 * ab + c for c in range(3)]
        for c, tile in enumerate(banded([one_ref[t] for t in taps])):
            one_out[ab, c] = tile
        for c, tile in enumerate(banded([flipped(two_ref, t) for t in taps])):
            two_flip_out[ab, c] = tile
        for c, tile in enumerate(banded([flipped(one_ref, t) for t in taps])):
            one_flip_out[ab, c] = tile


def prepare(kernel_one, kernel_two):
    shape = jax.ShapeDtypeStruct((9, 4, CH, 2 * CH), jnp.bfloat16)
    vmem = pl.BlockSpec(memory_space=pltpu.VMEM)
    hbm = pl.BlockSpec(memory_space=pltpu.HBM)
    return pl.pallas_call(
        prepare_kernel,
        out_shape=(shape, shape, shape),
        in_specs=[hbm, hbm],
        out_specs=(vmem, vmem, vmem),
        scratch_shapes=[pltpu.VMEM(kernel_one.shape, kernel_one.dtype)] * 2
        + [pltpu.SemaphoreType.DMA((2,))],
        compiler_params=pltpu.CompilerParams(vmem_limit_bytes=8 << 20),
        cost_estimate=pl.CostEstimate(
            flops=4_000_000, bytes_accessed=4_000_000, transcendentals=0
        ),
    )(in_hbm(kernel_one), in_hbm(kernel_two))


def banded_weights(band_ref, group):
    zero = jnp.zeros((CH, 2 * CH), jnp.bfloat16)
    lift = 1 if group == 0 else -1
    rows = []
    for ab in range(9):
        for i in range(6):
            halves = []
            for m in range(2):
                c = i - 2 * m + lift
                halves.append(band_ref[ab, c] if 0 <= c < 4 else zero)
            rows.append(jnp.concatenate(halves, axis=1))
    return jnp.concatenate(rows, axis=0)


def correlate(src, band_ref, start, count, stride):
    outs = []
    for group in range(2):
        lane = 128 * group
        windows = []
        for ab in range(9):
            top = start + (ab // 3 - 1) * stride
            windows.append(src[ab % 3, top : top + count, lane : lane + 6 * CH])
        outs.append(
            jnp.dot(
                jnp.concatenate(windows, axis=1),
                banded_weights(band_ref, group),
                preferred_element_type=jnp.float32,
            )
        )
    return outs


def input_grad_kernel(rows, cols, ps, band_ref, out_ref):
    stride = cols + PAD
    result = correlate(ps, band_ref, PAD + 2 * stride, (rows - 1) * stride + cols, stride)
    for group in range(2):
        for r in range(rows):
            out_ref[r, :, 256 * group : 256 * group + 256] = result[group][
                r * stride : r * stride + cols
            ].astype(out_ref.dtype)


def main_kernel(
    rows,
    cols,
    x_ref,
    g_ref,
    ra_ref,
    rb_ref,
    wa_ref,
    wb_ref,
    corner_a_ref,
    corner_b_ref,
    one_ref,
    two_flip_ref,
    ps,
    *rest,
):
    kg_refs, (wide, xs, gs, sums, acc_ref, turned, edges) = rest[:-7], rest[-7:]
    f32, bf16 = jnp.float32, jnp.bfloat16
    stride = cols + PAD
    lines = rows + 4
    span = lines * stride + PAD
    base = 8
    ha = lax.axis_index("ha")
    wa = lax.axis_index("wa")
    ha_odd = lax.rem(ha, 2)
    wa_odd = lax.rem(wa, 2)

    halo = 2 * lines
    gap_rows = (lines + 1) * PAD
    q = lax.broadcasted_iota(jnp.int32, (gap_rows, 2 * halo), 0)
    col = lax.broadcasted_iota(jnp.int32, (gap_rows, 2 * halo), 1)
    gap = lax.div(q, PAD)
    w = lax.rem(q, PAD)

    def order(line):
        swapped = jnp.where(
            line < 2, line + lines - 2, jnp.where(line >= lines - 2, line - lines + 2, line)
        )
        return jnp.where(ha_odd == 0, swapped, line)

    left_base = jnp.where(wa_odd == 0, halo, 0)
    right_base = jnp.where(wa_odd == 0, 0, halo)
    left_hit = (w >= PAD - 2) & (gap < lines) & (col == left_base + 2 * order(gap) + w - (PAD - 2))
    right_hit = (w < 2) & (gap >= 1) & (col == right_base + 2 * order(gap - 1) + w)
    select = jnp.where(left_hit | right_hit, 1.0, 0.0).astype(bf16)

    def spread(which, own_ref, out):
        for side, ref in enumerate((wa_ref, wb_ref)):
            pieces = (
                [corner_a_ref[side, which, r] for r in range(2)]
                + [ref[which, r] for r in range(rows)]
                + [corner_b_ref[side, which, r] for r in range(2)]
            )
            for k, piece in enumerate(pieces):
                at = side * halo + 2 * k
                edges[at : at + 2, :] = piece.astype(f32)
        gaps = jnp.dot(select, edges[...].astype(bf16), preferred_element_type=f32)
        for k in range(lines + 1):
            wide[base + k * stride : base + k * stride + PAD, :] = gaps[k * PAD : (k + 1) * PAD]
        for r in range(rows):
            start = base + PAD + (r + 2) * stride
            wide[start : start + cols, :] = own_ref[r].astype(f32)
        above = base + PAD
        below = base + PAD + (rows + 2) * stride
        a_start = jnp.where(ha_odd == 0, below, above)
        b_start = jnp.where(ha_odd == 0, above, below)
        for r in range(2):
            wide[pl.ds(pl.multiple_of(a_start + r * stride, 8), cols), :] = ra_ref[which, r].astype(f32)
            wide[pl.ds(pl.multiple_of(b_start + r * stride, 8), cols), :] = rb_ref[which, r].astype(f32)
        for b in range(3):
            out[b] = wide[base + b - 1 : base + b - 1 + span, :].astype(bf16)

    spread(0, x_ref, xs)
    spread(1, g_ref, gs)

    first = stride
    count = (rows + 2) * stride + PAD
    pre = correlate(xs, one_ref, first, count, stride)
    grad_active = correlate(gs, two_flip_ref, first, count, stride)

    position = first + lax.broadcasted_iota(jnp.int32, (count, 256), 0)
    line = lax.div(position, stride)
    w = lax.rem(position, stride)
    ha_last = lax.axis_size("ha") - 1
    wa_last = lax.axis_size("wa") - 1
    owner = jnp.where(w < PAD // 2, line - 1, line)
    dead = ((owner < 2) & (ha == 0)) | ((owner >= rows + 2) & (ha == ha_last))
    dead = dead | ((w >= PAD // 2) & (w < PAD) & (wa == 0)) | ((w < PAD // 2) & (wa == wa_last))

    def transposed(value):
        flat = jnp.transpose(value)
        halves = []
        for side in range(flat.shape[1] // 128):
            turned[side] = flat[:, 128 * side : 128 * side + 128]
            pieces = [
                turned[side, pl.ds(64 * j + odd, 32, stride=2), :]
                for j in range(4)
                for odd in range(2)
            ]
            halves.append(jnp.concatenate(pieces, axis=0))
        return jnp.concatenate(halves, axis=1).astype(bf16)

    own_line = [PAD + (r + 1) * stride for r in range(rows)]
    active_t = []
    for group in range(2):
        value = pre[group]
        cdf = 0.5 * (1.0 + lax.erf(value * root_half))
        slope = cdf + value * inv_root_two_pi * jnp.exp(-0.5 * value * value)
        grad_pre = jnp.where(dead, 0.0, grad_active[group] * slope)
        wide[base + first : base + first + count, 256 * group : 256 * group + 256] = (
            grad_pre.astype(bf16).astype(f32)
        )
        active = value * cdf
        active = jnp.concatenate([active[s : s + cols] for s in own_line], axis=0)
        active_t.append(transposed(active))
    for b in range(3):
        ps[b, first : first + count, :] = wide[
            base + first + b - 1 : base + first + b - 1 + count, :
        ].astype(bf16)

    x_own = jnp.concatenate([x_ref[r] for r in range(rows)], axis=0).astype(f32)
    x_t = [transposed(x_own[:, 256 * group : 256 * group + 256]) for group in range(2)]

    def kernel_grad(fixed, src, a):
        parts = [[[None] * 4 for _ in range(3)] for _ in range(1)][0]
        for group in range(2):
            lane = 128 * group
            windows = []
            for b in range(3):
                shift = (1 - a) * stride
                windows.append(
                    jnp.concatenate(
                        [
                            src[2 - b, PAD + (r + 2) * stride + shift : PAD + (r + 2) * stride + shift + cols, lane : lane + 6 * CH]
                            for r in range(rows)
                        ],
                        axis=0,
                    )
                )
            acc_ref[...] = jnp.dot(
                fixed[group], jnp.concatenate(windows, axis=1), preferred_element_type=f32
            )
            lift = 1 if group == 0 else 3
            for b in range(3):
                for j in range(4):
                    for m in range(3):
                        e = j - 2 * m + lift
                        if 0 <= e < 4:
                            tile = acc_ref[64 * j : 64 * j + 64, 384 * b + 128 * m : 384 * b + 128 * m + 128]
                            old = parts[b][e]
                            parts[b][e] = tile if old is None else old + tile
        return parts

    half = CH // 2
    low = lax.broadcasted_iota(jnp.int32, (half, 2 * CH), 1) < CH
    for a in range(3):
        for k, parts in enumerate((kernel_grad(x_t, ps, a), kernel_grad(active_t, gs, a))):
            for b in range(3):
                for c in range(3):
                    left, right = parts[b][c], parts[b][c + 1]
                    tile = jnp.where(
                        low,
                        left[:half] + pltpu.roll(right[:half], CH, 1),
                        pltpu.roll(left[half:], CH, 1) + right[half:],
                    )
                    tap = 9 * a + 3 * b + c
                    sums[k, half * tap : half * tap + half, :] = tile
    if len(kg_refs) == 1:
        for k in range(2):
            kg_refs[0][k] = sums[k, : 27 * half, :]
        return
    keep_ref, send_ref = kg_refs
    slabs, width, _, share, _ = keep_ref.shape
    take = 27 * half // (2 * slabs * width)
    for z in range(slabs):
        for w in range(width):
            for k in range(2):
                at = [take * ((2 * z + c) * width + w) for c in range(2)]
                even, odd = (sums[k, r : r + share, :] for r in at)
                keep_ref[z, w, k] = jnp.where(ha_odd == 0, even, odd)
                send_ref[z, w, k] = jnp.where(ha_odd == 0, odd, even).astype(bf16)


def main(x, g, ra, rb, wa, wb, corner_a, corner_b, one, two_flip, split):
    rows, cols, lanes = x.shape
    stride = cols + PAD
    span = (rows + 4) * stride + PAD
    if split:
        slabs, width = split
        take = 27 * CH // 2 // (2 * slabs * width)
        share = -(-take // 8) * 8
        grads = tuple(
            jax.ShapeDtypeStruct((slabs, width, 2, share, 2 * CH), dtype)
            for dtype in (jnp.float32, jnp.bfloat16)
        )
    else:
        grads = (jax.ShapeDtypeStruct((2, 27 * CH // 2, 2 * CH), jnp.float32),)
    vmem = pl.BlockSpec(memory_space=pltpu.VMEM)
    moving = pltpu.VMEM((3, span, lanes), jnp.bfloat16)
    return pl.pallas_call(
        functools.partial(main_kernel, rows, cols),
        out_shape=(
            jax.ShapeDtypeStruct((3, span, lanes), jnp.bfloat16),
            *grads,
        ),
        in_specs=[vmem] * 10,
        out_specs=(vmem,) * (1 + len(grads)),
        scratch_shapes=[
            pltpu.VMEM((span + 16, lanes), jnp.float32),
            moving,
            moving,
            pltpu.VMEM((2, 27 * CH // 2 + 8, 2 * CH), jnp.float32),
            pltpu.VMEM((256, 1152), jnp.float32),
            pltpu.VMEM((rows * cols // 128, 256, 128), jnp.float32),
            pltpu.VMEM((4 * (rows + 4), lanes), jnp.float32),
        ],
        compiler_params=pltpu.CompilerParams(vmem_limit_bytes=16 << 20),
        cost_estimate=pl.CostEstimate(
            flops=14_000_000_000, bytes_accessed=8_000_000, transcendentals=1_000_000
        ),
    )(x, g, ra, rb, wa, wb, corner_a, corner_b, one, two_flip)


def input_grad(ps, band, shape):
    rows, cols, _ = shape
    vmem = pl.BlockSpec(memory_space=pltpu.VMEM)
    return pl.pallas_call(
        functools.partial(input_grad_kernel, rows, cols),
        out_shape=jax.ShapeDtypeStruct(shape, jnp.bfloat16),
        in_specs=[vmem, vmem],
        out_specs=vmem,
        compiler_params=pltpu.CompilerParams(vmem_limit_bytes=8 << 20),
        cost_estimate=pl.CostEstimate(
            flops=2_000_000_000, bytes_accessed=4_000_000, transcendentals=0
        ),
    )(ps, band)


def xor_exchange(block, axis, mask):
    count = lax.axis_size(axis)
    return lax.ppermute(block, axis, [(i, i ^ mask) for i in range(count)])


def total_of(refs):
    total = refs[0].astype(jnp.float32)
    for ref in refs[1:]:
        total = total + ref.astype(jnp.float32)
    return total


def sum_chip_kernel(keep_ref, got_ref, own_ref, *send_refs):
    wa = lax.axis_index("wa")
    for z in range(keep_ref.shape[0]):
        own_ref[z] = total_of([keep_ref[z, wa], got_ref[z, wa]])
        for k, ref in enumerate(send_refs, 1):
            ref[z] = total_of([keep_ref[z, wa ^ k], got_ref[z, wa ^ k]]).astype(ref.dtype)


def sum_wa_kernel(*refs):
    slabs = refs[0].shape[0]
    got_refs, (own_ref, *send_refs) = refs[:-slabs], refs[-slabs:]
    z = lax.div(lax.axis_index("ha"), 2)
    own_ref[...] = total_of([ref[z] for ref in got_refs])
    for k, ref in enumerate(send_refs, 1):
        ref[...] = total_of([got[z ^ k] for got in got_refs])


def sum_z_kernel(*refs):
    total = total_of([ref[...] for ref in refs[:-2]])
    take = refs[-1].shape[0]
    for k, ref in enumerate(refs[-2:]):
        ref[...] = total[k, :take]


def reduce_chunks(keep, send, take):
    slabs, width = keep.shape[:2]
    f32, bf16 = jnp.float32, jnp.bfloat16
    unit = keep.shape[2:]
    got = xor_exchange(send, "ha", 1)
    shapes = [jax.ShapeDtypeStruct((slabs,) + unit, f32)]
    shapes += [jax.ShapeDtypeStruct((slabs,) + unit, bf16)] * (width - 1)
    own, *sends = small_call(sum_chip_kernel, tuple(shapes), keep, got)
    got = [xor_exchange(block, "wa", k) for k, block in enumerate(sends, 1)]
    shapes = [jax.ShapeDtypeStruct(unit, f32)] * slabs
    own, *sends = small_call(sum_wa_kernel, tuple(shapes), own, *got)
    got = [xor_exchange(block, "ha", 2 * k) for k, block in enumerate(sends, 1)]
    shapes = (jax.ShapeDtypeStruct((take, 2 * CH), f32),) * 2
    return small_call(sum_z_kernel, shapes, own, *got)


def shards(inputs, grad_out, kernel_one, kernel_two):
    height_count = lax.axis_size("ha")
    width_count = lax.axis_size("wa")
    devices = height_count * width_count
    x, g, to_a, to_b, own_a, own_b = pack(inputs, grad_out)
    wb = pair_exchange(own_b, "wa", 1)
    wa = pair_exchange(own_a, "wa", 0)
    ra = pair_exchange(to_a, "ha", 0)
    rb = pair_exchange(to_b, "ha", 1)
    one, two_flip, one_flip = prepare(kernel_one, kernel_two)
    corner_to_a, corner_to_b = corners(wa, wb)
    corner_b = pair_exchange(corner_to_b, "ha", 1)
    corner_a = pair_exchange(corner_to_a, "ha", 0)

    split = None
    if (
        (27 * CH // 2) % devices == 0
        and height_count & (height_count - 1) == 0
        and width_count & (width_count - 1) == 0
        and height_count > 1
    ):
        split = (height_count // 2, width_count)
    ps, *grads = main(x, g, ra, rb, wa, wb, corner_a, corner_b, one, two_flip, split)
    grad_inputs = input_grad(ps, one_flip, inputs.shape)
    if split:
        grads = reduce_chunks(*grads, 27 * CH // 2 // devices)
    else:
        grads = [
            lax.psum_scatter(
                grads[0][k].reshape(devices, -1), ("ha", "wa"), scatter_dimension=0, tiled=True
            )
            for k in range(2)
        ]
    return (grad_inputs, grads[0].reshape(-1), grads[1].reshape(-1))


def solution(mesh):
    return jax.shard_map(
        shards,
        mesh=mesh,
        in_specs=(P("ha", "wa", None), P("ha", "wa", None), P(), P()),
        out_specs=(P("ha", "wa", None), P(("ha", "wa")), P(("ha", "wa"))),
        check_vma=False,
    )
```

```python
import functools

import jax
import jax.numpy as jnp
from jax import lax
from jax.experimental import pallas as pl
from jax.experimental.pallas import tpu as pltpu
from jax.sharding import PartitionSpec as P


CH = 64
PAD = 16

root_half = 0.7071067811865476
inv_root_two_pi = 0.3989422804014327


def pair_exchange(block, axis, first):
    count = lax.axis_size(axis)
    pairs = []
    for low in range(first, count - 1, 2):
        pairs += [(low, low + 1), (low + 1, low)]
    return lax.ppermute(block, axis, pairs)


def in_hbm(block):
    return pltpu.with_memory_space_constraint(block, pltpu.HBM)


def pack_kernel(
    x_hbm, g_hbm, one_hbm, two_hbm, x_ref, g_ref, one_ref, two_ref, to_a, to_b, own_a, own_b, sems
):
    rows, cols, _ = x_ref.shape
    pairs = ((x_hbm, x_ref), (g_hbm, g_ref), (one_hbm, one_ref), (two_hbm, two_ref))
    copies = [
        pltpu.make_async_copy(source, target, sems.at[k])
        for k, (source, target) in enumerate(pairs)
    ]
    for copy in copies:
        copy.start()
    ha_even = lax.rem(lax.axis_index("ha"), 2) == 0
    wa_even = lax.rem(lax.axis_index("wa"), 2) == 0
    a_start = jnp.where(ha_even, rows - 2, 0)
    b_start = jnp.where(ha_even, 0, rows - 2)
    for which, ref in enumerate((x_ref, g_ref)):
        copies[which].wait()
        to_a[which] = ref[pl.ds(a_start, 2)]
        to_b[which] = ref[pl.ds(b_start, 2)]
        for r in range(rows):
            left, right = ref[r, 0:2, :], ref[r, cols - 2 : cols, :]
            own_a[which, r] = jnp.where(wa_even, right, left)
            own_b[which, r] = jnp.where(wa_even, left, right)
    for copy in copies[2:]:
        copy.wait()


def pack(x, g, one, two):
    rows, cols, lanes = x.shape
    vmem = pl.BlockSpec(memory_space=pltpu.VMEM)
    hbm = pl.BlockSpec(memory_space=pltpu.HBM)
    shapes = [x.shape] * 2 + [one.shape] * 2
    shapes += [(2, 2, cols, lanes)] * 2 + [(2, rows, 2, lanes)] * 2
    return pl.pallas_call(
        pack_kernel,
        out_shape=tuple(jax.ShapeDtypeStruct(shape, x.dtype) for shape in shapes),
        in_specs=[hbm] * 4,
        out_specs=(vmem,) * 8,
        scratch_shapes=[pltpu.SemaphoreType.DMA((4,))],
        compiler_params=pltpu.CompilerParams(vmem_limit_bytes=4 << 20),
        cost_estimate=pl.CostEstimate(flops=0, bytes_accessed=1_100_000, transcendentals=0),
    )(*(in_hbm(block) for block in (x, g, one, two)))


def corners_kernel(wa_ref, wb_ref, to_a, to_b):
    rows = wa_ref.shape[1]
    ha_even = lax.rem(lax.axis_index("ha"), 2) == 0
    a_start = jnp.where(ha_even, rows - 2, 0)
    b_start = jnp.where(ha_even, 0, rows - 2)
    for side, ref in enumerate((wa_ref, wb_ref)):
        for which in range(2):
            for r in range(2):
                to_a[side, which, r] = ref[which, a_start + r]
                to_b[side, which, r] = ref[which, b_start + r]


def small_call(kernel, out_shape, *operands):
    vmem = pl.BlockSpec(memory_space=pltpu.VMEM)
    return pl.pallas_call(
        kernel,
        out_shape=out_shape,
        in_specs=[vmem] * len(operands),
        out_specs=(vmem,) * len(out_shape),
        compiler_params=pltpu.CompilerParams(vmem_limit_bytes=2 << 20),
        cost_estimate=pl.CostEstimate(flops=0, bytes_accessed=300_000, transcendentals=0),
    )(*operands)


def corners(wa, wb):
    shape = jax.ShapeDtypeStruct((2, 2, 2) + wa.shape[2:], wa.dtype)
    return small_call(corners_kernel, (shape, shape), wa, wb)


def prepare_kernel(one_ref, two_ref, one_out, two_flip_out, one_flip_out):
    zero = jnp.zeros((CH, CH), jnp.bfloat16)

    def banded(tiles):
        padded = [zero] + tiles + [zero]
        return [jnp.concatenate([padded[c + 1], padded[c]], axis=1) for c in range(4)]

    def flipped(ref, tap):
        return jnp.transpose(ref[26 - tap].astype(jnp.float32)).astype(jnp.bfloat16)

    for ab in range(9):
        taps = [3 * ab + c for c in range(3)]
        for c, tile in enumerate(banded([one_ref[t] for t in taps])):
            one_out[ab, c] = tile
        for c, tile in enumerate(banded([flipped(two_ref, t) for t in taps])):
            two_flip_out[ab, c] = tile
        for c, tile in enumerate(banded([flipped(one_ref, t) for t in taps])):
            one_flip_out[ab, c] = tile


def prepare(kernel_one, kernel_two):
    shape = jax.ShapeDtypeStruct((9, 4, CH, 2 * CH), jnp.bfloat16)
    vmem = pl.BlockSpec(memory_space=pltpu.VMEM)
    return pl.pallas_call(
        prepare_kernel,
        out_shape=(shape, shape, shape),
        in_specs=[vmem, vmem],
        out_specs=(vmem, vmem, vmem),
        compiler_params=pltpu.CompilerParams(vmem_limit_bytes=8 << 20),
        cost_estimate=pl.CostEstimate(
            flops=4_000_000, bytes_accessed=4_000_000, transcendentals=0
        ),
    )(kernel_one, kernel_two)


def banded_weights(band_ref, group):
    zero = jnp.zeros((CH, 2 * CH), jnp.bfloat16)
    lift = 1 if group == 0 else -1
    rows = []
    for ab in range(9):
        for i in range(6):
            halves = []
            for m in range(2):
                c = i - 2 * m + lift
                halves.append(band_ref[ab, c] if 0 <= c < 4 else zero)
            rows.append(jnp.concatenate(halves, axis=1))
    return jnp.concatenate(rows, axis=0)


def correlate(src, band_ref, start, count, stride):
    outs = []
    for group in range(2):
        lane = 128 * group
        windows = []
        for ab in range(9):
            top = start + (ab // 3 - 1) * stride
            windows.append(src[ab % 3, top : top + count, lane : lane + 6 * CH])
        outs.append(
            jnp.dot(
                jnp.concatenate(windows, axis=1),
                banded_weights(band_ref, group),
                preferred_element_type=jnp.float32,
            )
        )
    return outs


def input_grad_kernel(rows, cols, ps, band_ref, out_ref):
    stride = cols + PAD
    result = correlate(ps, band_ref, PAD + 2 * stride, (rows - 1) * stride + cols, stride)
    for group in range(2):
        for r in range(rows):
            out_ref[r, :, 256 * group : 256 * group + 256] = result[group][
                r * stride : r * stride + cols
            ].astype(out_ref.dtype)


def main_kernel(
    rows,
    cols,
    x_ref,
    g_ref,
    ra_ref,
    rb_ref,
    wa_ref,
    wb_ref,
    corner_a_ref,
    corner_b_ref,
    one_ref,
    two_flip_ref,
    ps,
    *rest,
):
    kg_refs, (wide, xs, gs, sums, acc_ref, turned, edges) = rest[:-7], rest[-7:]
    f32, bf16 = jnp.float32, jnp.bfloat16
    stride = cols + PAD
    lines = rows + 4
    span = lines * stride + PAD
    base = 8
    ha = lax.axis_index("ha")
    wa = lax.axis_index("wa")
    ha_odd = lax.rem(ha, 2)
    wa_odd = lax.rem(wa, 2)

    halo = 2 * lines
    gap_rows = (lines + 1) * PAD
    q = lax.broadcasted_iota(jnp.int32, (gap_rows, 2 * halo), 0)
    col = lax.broadcasted_iota(jnp.int32, (gap_rows, 2 * halo), 1)
    gap = lax.div(q, PAD)
    w = lax.rem(q, PAD)

    def order(line):
        swapped = jnp.where(
            line < 2, line + lines - 2, jnp.where(line >= lines - 2, line - lines + 2, line)
        )
        return jnp.where(ha_odd == 0, swapped, line)

    left_base = jnp.where(wa_odd == 0, halo, 0)
    right_base = jnp.where(wa_odd == 0, 0, halo)
    left_hit = (w >= PAD - 2) & (gap < lines) & (col == left_base + 2 * order(gap) + w - (PAD - 2))
    right_hit = (w < 2) & (gap >= 1) & (col == right_base + 2 * order(gap - 1) + w)
    select = jnp.where(left_hit | right_hit, 1.0, 0.0).astype(bf16)

    def spread(which, own_ref, out):
        for side, ref in enumerate((wa_ref, wb_ref)):
            pieces = (
                [corner_a_ref[side, which, r] for r in range(2)]
                + [ref[which, r] for r in range(rows)]
                + [corner_b_ref[side, which, r] for r in range(2)]
            )
            for k, piece in enumerate(pieces):
                at = side * halo + 2 * k
                edges[at : at + 2, :] = piece.astype(f32)
        gaps = jnp.dot(select, edges[...].astype(bf16), preferred_element_type=f32)
        for k in range(lines + 1):
            wide[base + k * stride : base + k * stride + PAD, :] = gaps[k * PAD : (k + 1) * PAD]
        for r in range(rows):
            start = base + PAD + (r + 2) * stride
            wide[start : start + cols, :] = own_ref[r].astype(f32)
        above = base + PAD
        below = base + PAD + (rows + 2) * stride
        a_start = jnp.where(ha_odd == 0, below, above)
        b_start = jnp.where(ha_odd == 0, above, below)
        for r in range(2):
            wide[pl.ds(pl.multiple_of(a_start + r * stride, 8), cols), :] = ra_ref[which, r].astype(f32)
            wide[pl.ds(pl.multiple_of(b_start + r * stride, 8), cols), :] = rb_ref[which, r].astype(f32)
        for b in range(3):
            out[b] = wide[base + b - 1 : base + b - 1 + span, :].astype(bf16)

    spread(0, x_ref, xs)
    spread(1, g_ref, gs)

    first = stride
    count = (rows + 2) * stride + PAD
    pre = correlate(xs, one_ref, first, count, stride)
    grad_active = correlate(gs, two_flip_ref, first, count, stride)

    position = first + lax.broadcasted_iota(jnp.int32, (count, 256), 0)
    line = lax.div(position, stride)
    w = lax.rem(position, stride)
    ha_last = lax.axis_size("ha") - 1
    wa_last = lax.axis_size("wa") - 1
    owner = jnp.where(w < PAD // 2, line - 1, line)
    dead = ((owner < 2) & (ha == 0)) | ((owner >= rows + 2) & (ha == ha_last))
    dead = dead | ((w >= PAD // 2) & (w < PAD) & (wa == 0)) | ((w < PAD // 2) & (wa == wa_last))

    def transposed(value):
        flat = jnp.transpose(value)
        halves = []
        for side in range(flat.shape[1] // 128):
            turned[side] = flat[:, 128 * side : 128 * side + 128]
            pieces = [
                turned[side, pl.ds(64 * j + odd, 32, stride=2), :]
                for j in range(4)
                for odd in range(2)
            ]
            halves.append(jnp.concatenate(pieces, axis=0))
        return jnp.concatenate(halves, axis=1).astype(bf16)

    own_line = [PAD + (r + 1) * stride for r in range(rows)]
    active_t = []
    for group in range(2):
        value = pre[group]
        cdf = 0.5 * (1.0 + lax.erf(value * root_half))
        slope = cdf + value * inv_root_two_pi * jnp.exp(-0.5 * value * value)
        grad_pre = jnp.where(dead, 0.0, grad_active[group] * slope)
        wide[base + first : base + first + count, 256 * group : 256 * group + 256] = (
            grad_pre.astype(bf16).astype(f32)
        )
        active = value * cdf
        active = jnp.concatenate([active[s : s + cols] for s in own_line], axis=0)
        active_t.append(transposed(active))
    for b in range(3):
        ps[b, first : first + count, :] = wide[
            base + first + b - 1 : base + first + b - 1 + count, :
        ].astype(bf16)

    x_own = jnp.concatenate([x_ref[r] for r in range(rows)], axis=0).astype(f32)
    x_t = [transposed(x_own[:, 256 * group : 256 * group + 256]) for group in range(2)]

    def kernel_grad(fixed, src, a):
        parts = [[[None] * 4 for _ in range(3)] for _ in range(1)][0]
        for group in range(2):
            lane = 128 * group
            windows = []
            for b in range(3):
                shift = (1 - a) * stride
                windows.append(
                    jnp.concatenate(
                        [
                            src[2 - b, PAD + (r + 2) * stride + shift : PAD + (r + 2) * stride + shift + cols, lane : lane + 6 * CH]
                            for r in range(rows)
                        ],
                        axis=0,
                    )
                )
            acc_ref[...] = jnp.dot(
                fixed[group], jnp.concatenate(windows, axis=1), preferred_element_type=f32
            )
            lift = 1 if group == 0 else 3
            for b in range(3):
                for j in range(4):
                    for m in range(3):
                        e = j - 2 * m + lift
                        if 0 <= e < 4:
                            tile = acc_ref[64 * j : 64 * j + 64, 384 * b + 128 * m : 384 * b + 128 * m + 128]
                            old = parts[b][e]
                            parts[b][e] = tile if old is None else old + tile
        return parts

    half = CH // 2
    low = lax.broadcasted_iota(jnp.int32, (half, 2 * CH), 1) < CH
    for a in range(3):
        for k, parts in enumerate((kernel_grad(x_t, ps, a), kernel_grad(active_t, gs, a))):
            for b in range(3):
                for c in range(3):
                    left, right = parts[b][c], parts[b][c + 1]
                    tile = jnp.where(
                        low,
                        left[:half] + pltpu.roll(right[:half], CH, 1),
                        pltpu.roll(left[half:], CH, 1) + right[half:],
                    )
                    tap = 9 * a + 3 * b + c
                    sums[k, half * tap : half * tap + half, :] = tile
    if len(kg_refs) == 1:
        for k in range(2):
            kg_refs[0][k] = sums[k, : 27 * half, :]
        return
    keep_ref, send_ref = kg_refs
    slabs, width, _, share, _ = keep_ref.shape
    take = 27 * half // (2 * slabs * width)
    for z in range(slabs):
        for w in range(width):
            for k in range(2):
                at = [take * ((2 * z + c) * width + w) for c in range(2)]
                even, odd = (sums[k, r : r + share, :] for r in at)
                keep_ref[z, w, k] = jnp.where(ha_odd == 0, even, odd)
                send_ref[z, w, k] = jnp.where(ha_odd == 0, odd, even).astype(bf16)


def main(x, g, ra, rb, wa, wb, corner_a, corner_b, one, two_flip, split):
    rows, cols, lanes = x.shape
    stride = cols + PAD
    span = (rows + 4) * stride + PAD
    if split:
        slabs, width = split
        take = 27 * CH // 2 // (2 * slabs * width)
        share = -(-take // 8) * 8
        grads = tuple(
            jax.ShapeDtypeStruct((slabs, width, 2, share, 2 * CH), dtype)
            for dtype in (jnp.float32, jnp.bfloat16)
        )
    else:
        grads = (jax.ShapeDtypeStruct((2, 27 * CH // 2, 2 * CH), jnp.float32),)
    vmem = pl.BlockSpec(memory_space=pltpu.VMEM)
    moving = pltpu.VMEM((3, span, lanes), jnp.bfloat16)
    return pl.pallas_call(
        functools.partial(main_kernel, rows, cols),
        out_shape=(
            jax.ShapeDtypeStruct((3, span, lanes), jnp.bfloat16),
            *grads,
        ),
        in_specs=[vmem] * 10,
        out_specs=(vmem,) * (1 + len(grads)),
        scratch_shapes=[
            pltpu.VMEM((span + 16, lanes), jnp.float32),
            moving,
            moving,
            pltpu.VMEM((2, 27 * CH // 2 + 8, 2 * CH), jnp.float32),
            pltpu.VMEM((256, 1152), jnp.float32),
            pltpu.VMEM((rows * cols // 128, 256, 128), jnp.float32),
            pltpu.VMEM((4 * (rows + 4), lanes), jnp.float32),
        ],
        compiler_params=pltpu.CompilerParams(vmem_limit_bytes=16 << 20),
        cost_estimate=pl.CostEstimate(
            flops=14_000_000_000, bytes_accessed=8_000_000, transcendentals=1_000_000
        ),
    )(x, g, ra, rb, wa, wb, corner_a, corner_b, one, two_flip)


def input_grad(ps, band, shape):
    rows, cols, _ = shape
    vmem = pl.BlockSpec(memory_space=pltpu.VMEM)
    return pl.pallas_call(
        functools.partial(input_grad_kernel, rows, cols),
        out_shape=jax.ShapeDtypeStruct(shape, jnp.bfloat16),
        in_specs=[vmem, vmem],
        out_specs=vmem,
        compiler_params=pltpu.CompilerParams(vmem_limit_bytes=8 << 20),
        cost_estimate=pl.CostEstimate(
            flops=2_000_000_000, bytes_accessed=4_000_000, transcendentals=0
        ),
    )(ps, band)


def xor_exchange(block, axis, mask):
    count = lax.axis_size(axis)
    return lax.ppermute(block, axis, [(i, i ^ mask) for i in range(count)])


def total_of(refs):
    total = refs[0].astype(jnp.float32)
    for ref in refs[1:]:
        total = total + ref.astype(jnp.float32)
    return total


def sum_chip_kernel(keep_ref, got_ref, own_ref, *send_refs):
    wa = lax.axis_index("wa")
    for z in range(keep_ref.shape[0]):
        own_ref[z] = total_of([keep_ref[z, wa], got_ref[z, wa]])
        for k, ref in enumerate(send_refs, 1):
            ref[z] = total_of([keep_ref[z, wa ^ k], got_ref[z, wa ^ k]]).astype(ref.dtype)


def sum_wa_kernel(*refs):
    slabs = refs[0].shape[0]
    got_refs, (own_ref, *send_refs) = refs[:-slabs], refs[-slabs:]
    z = lax.div(lax.axis_index("ha"), 2)
    own_ref[...] = total_of([ref[z] for ref in got_refs])
    for k, ref in enumerate(send_refs, 1):
        ref[...] = total_of([got[z ^ k] for got in got_refs])


def sum_z_kernel(*refs):
    total = total_of([ref[...] for ref in refs[:-2]])
    take = refs[-1].shape[0]
    for k, ref in enumerate(refs[-2:]):
        ref[...] = total[k, :take]


def reduce_chunks(keep, send, take):
    slabs, width = keep.shape[:2]
    f32, bf16 = jnp.float32, jnp.bfloat16
    unit = keep.shape[2:]
    got = xor_exchange(send, "ha", 1)
    shapes = [jax.ShapeDtypeStruct((slabs,) + unit, f32)]
    shapes += [jax.ShapeDtypeStruct((slabs,) + unit, bf16)] * (width - 1)
    own, *sends = small_call(sum_chip_kernel, tuple(shapes), keep, got)
    got = []
    for k, block in enumerate(sends, 1):
        got.append(xor_exchange(block, "wa", k))
    shapes = [jax.ShapeDtypeStruct(unit, f32)] * slabs
    own, *sends = small_call(sum_wa_kernel, tuple(shapes), own, *got)
    got = []
    for k, block in enumerate(sends, 1):
        got.append(xor_exchange(block, "ha", 2 * k))
    shapes = (jax.ShapeDtypeStruct((take, 2 * CH), f32),) * 2
    return small_call(sum_z_kernel, shapes, own, *got)


def shards(inputs, grad_out, kernel_one, kernel_two):
    height_count = lax.axis_size("ha")
    width_count = lax.axis_size("wa")
    devices = height_count * width_count
    x, g, kernel_one, kernel_two, to_a, to_b, own_a, own_b = pack(
        inputs, grad_out, kernel_one, kernel_two
    )
    wb = pair_exchange(own_b, "wa", 1)
    wa = pair_exchange(own_a, "wa", 0)
    ra = pair_exchange(to_a, "ha", 0)
    rb = pair_exchange(to_b, "ha", 1)
    one, two_flip, one_flip = prepare(kernel_one, kernel_two)
    corner_to_a, corner_to_b = corners(wa, wb)
    corner_b = pair_exchange(corner_to_b, "ha", 1)
    corner_a = pair_exchange(corner_to_a, "ha", 0)

    split = None
    if (
        (27 * CH // 2) % devices == 0
        and height_count & (height_count - 1) == 0
        and width_count & (width_count - 1) == 0
        and height_count > 1
    ):
        split = (height_count // 2, width_count)
    ps, *grads = main(x, g, ra, rb, wa, wb, corner_a, corner_b, one, two_flip, split)
    grad_inputs = input_grad(ps, one_flip, inputs.shape)
    if split:
        grads = reduce_chunks(*grads, 27 * CH // 2 // devices)
    else:
        grads = [
            lax.psum_scatter(
                grads[0][k].reshape(devices, -1), ("ha", "wa"), scatter_dimension=0, tiled=True
            )
            for k in range(2)
        ]
    return (grad_inputs, grads[0].reshape(-1), grads[1].reshape(-1))


def solution(mesh):
    return jax.shard_map(
        shards,
        mesh=mesh,
        in_specs=(P("ha", "wa", None), P("ha", "wa", None), P(), P()),
        out_specs=(P("ha", "wa", None), P(("ha", "wa")), P(("ha", "wa"))),
        check_vma=False,
    )
```

```python
import functools

import jax
import jax.numpy as jnp
from jax import lax
from jax.experimental import pallas as pl
from jax.experimental.pallas import tpu as pltpu
from jax.sharding import PartitionSpec as P


CH = 64
PAD = 16

root_half = 0.7071067811865476
inv_root_two_pi = 0.3989422804014327


def pair_exchange(block, axis, first):
    count = lax.axis_size(axis)
    pairs = []
    for low in range(first, count - 1, 2):
        pairs += [(low, low + 1), (low + 1, low)]
    return lax.ppermute(block, axis, pairs)


def in_hbm(block):
    return pltpu.with_memory_space_constraint(block, pltpu.HBM)


def pack_kernel(
    x_hbm, g_hbm, one_hbm, two_hbm, x_ref, g_ref, one_ref, two_ref, to_a, to_b, own_a, own_b, sems
):
    rows, cols, _ = x_ref.shape
    pairs = ((x_hbm, x_ref), (g_hbm, g_ref), (one_hbm, one_ref), (two_hbm, two_ref))
    copies = [
        pltpu.make_async_copy(source, target, sems.at[k])
        for k, (source, target) in enumerate(pairs)
    ]
    for copy in copies:
        copy.start()
    ha_even = lax.rem(lax.axis_index("ha"), 2) == 0
    wa_even = lax.rem(lax.axis_index("wa"), 2) == 0
    a_start = jnp.where(ha_even, rows - 2, 0)
    b_start = jnp.where(ha_even, 0, rows - 2)
    for which, ref in enumerate((x_ref, g_ref)):
        copies[which].wait()
        to_a[which] = ref[pl.ds(a_start, 2)]
        to_b[which] = ref[pl.ds(b_start, 2)]
        for r in range(rows):
            left, right = ref[r, 0:2, :], ref[r, cols - 2 : cols, :]
            own_a[which, r] = jnp.where(wa_even, right, left)
            own_b[which, r] = jnp.where(wa_even, left, right)
    for copy in copies[2:]:
        copy.wait()


def pack(x, g, one, two):
    rows, cols, lanes = x.shape
    vmem = pl.BlockSpec(memory_space=pltpu.VMEM)
    hbm = pl.BlockSpec(memory_space=pltpu.HBM)
    shapes = [x.shape] * 2 + [one.shape] * 2
    shapes += [(2, 2, cols, lanes)] * 2 + [(2, rows, 2, lanes)] * 2
    return pl.pallas_call(
        pack_kernel,
        out_shape=tuple(jax.ShapeDtypeStruct(shape, x.dtype) for shape in shapes),
        in_specs=[hbm] * 4,
        out_specs=(vmem,) * 8,
        scratch_shapes=[pltpu.SemaphoreType.DMA((4,))],
        compiler_params=pltpu.CompilerParams(vmem_limit_bytes=4 << 20),
        cost_estimate=pl.CostEstimate(flops=0, bytes_accessed=1_100_000, transcendentals=0),
    )(*(in_hbm(block) for block in (x, g, one, two)))


def corners_kernel(wa_ref, wb_ref, to_a, to_b):
    rows = wa_ref.shape[1]
    ha_even = lax.rem(lax.axis_index("ha"), 2) == 0
    a_start = jnp.where(ha_even, rows - 2, 0)
    b_start = jnp.where(ha_even, 0, rows - 2)
    for side, ref in enumerate((wa_ref, wb_ref)):
        for which in range(2):
            for r in range(2):
                to_a[side, which, r] = ref[which, a_start + r]
                to_b[side, which, r] = ref[which, b_start + r]


def small_call(kernel, out_shape, *operands):
    vmem = pl.BlockSpec(memory_space=pltpu.VMEM)
    return pl.pallas_call(
        kernel,
        out_shape=out_shape,
        in_specs=[vmem] * len(operands),
        out_specs=(vmem,) * len(out_shape),
        compiler_params=pltpu.CompilerParams(vmem_limit_bytes=2 << 20),
        cost_estimate=pl.CostEstimate(flops=0, bytes_accessed=300_000, transcendentals=0),
    )(*operands)


def corners(wa, wb):
    shape = jax.ShapeDtypeStruct((2, 2, 2) + wa.shape[2:], wa.dtype)
    return small_call(corners_kernel, (shape, shape), wa, wb)


def halo_selection(lines, shape):
    ha_odd = lax.rem(lax.axis_index("ha"), 2)
    wa_odd = lax.rem(lax.axis_index("wa"), 2)
    halo = 2 * lines
    gap_rows = (lines + 1) * PAD
    side_rows = 2 * lines
    q = lax.broadcasted_iota(jnp.int32, shape, 0)
    col = lax.broadcasted_iota(jnp.int32, shape, 1)

    def order(line):
        swapped = jnp.where(
            line < 2, line + lines - 2, jnp.where(line >= lines - 2, line - lines + 2, line)
        )
        return jnp.where(ha_odd == 0, swapped, line)

    left_base = jnp.where(wa_odd == 0, halo, 0)
    right_base = jnp.where(wa_odd == 0, 0, halo)
    gap = lax.div(q, PAD)
    w = lax.rem(q, PAD)
    left_hit = (w == PAD - 1) & (gap < lines) & (col == left_base + 2 * order(gap) + 1)
    right_hit = (w == 0) & (gap >= 1) & (col == right_base + 2 * order(gap - 1))
    in_gaps = (q < gap_rows) & (left_hit | right_hit)
    q = q - gap_rows
    tap = lax.div(q, side_rows)
    b = lax.rem(tap, 3)
    right = lax.div(lax.rem(q, side_rows), lines)
    line = lax.rem(q, lines) + lax.div(tap, 3) - 1
    at = order(line)
    left_source = jnp.where(b == 2, 2 * halo + at, left_base + 2 * at + b)
    right_source = jnp.where(b == 0, 2 * halo + lines + at, right_base + 2 * at + b - 1)
    source = jnp.where(right == 0, left_source, right_source)
    in_sides = (q >= 0) & (line >= 0) & (line < lines) & (col == source)
    return jnp.where(in_gaps | in_sides, 1.0, 0.0).astype(jnp.bfloat16)


def transposed(value, turned):
    flat = jnp.transpose(value)
    halves = []
    for side in range(flat.shape[1] // 128):
        turned[side] = flat[:, 128 * side : 128 * side + 128]
        pieces = [
            turned[side, pl.ds(64 * j + odd, 32, stride=2), :] for j in range(4) for odd in range(2)
        ]
        halves.append(jnp.concatenate(pieces, axis=0))
    return jnp.concatenate(halves, axis=1).astype(jnp.bfloat16)


def prepare_kernel(
    x_ref, one_ref, two_ref, one_out, two_flip_out, one_flip_out, select_out, x_t_out, turned
):
    rows = x_ref.shape[0]
    select_out[...] = halo_selection(rows + 4, select_out.shape)
    for group in range(2):
        lane = slice(256 * group, 256 * group + 256)
        own = jnp.concatenate([x_ref[r, :, lane] for r in range(rows)], axis=0)
        x_t_out[group] = transposed(own.astype(jnp.float32), turned)
    zero = jnp.zeros((CH, CH), jnp.bfloat16)

    def banded(tiles):
        padded = [zero] + tiles + [zero]
        return [jnp.concatenate([padded[c + 1], padded[c]], axis=1) for c in range(4)]

    def flipped(ref, tap):
        return jnp.transpose(ref[26 - tap].astype(jnp.float32)).astype(jnp.bfloat16)

    for ab in range(9):
        taps = [3 * ab + c for c in range(3)]
        for c, tile in enumerate(banded([one_ref[t] for t in taps])):
            one_out[ab, c] = tile
        for c, tile in enumerate(banded([flipped(two_ref, t) for t in taps])):
            two_flip_out[ab, c] = tile
        for c, tile in enumerate(banded([flipped(one_ref, t) for t in taps])):
            one_flip_out[ab, c] = tile


def prepare(x, kernel_one, kernel_two):
    rows, cols, _ = x.shape
    lines = rows + 4
    bands = jax.ShapeDtypeStruct((9, 4, CH, 2 * CH), jnp.bfloat16)
    select = ((lines + 1) * PAD + 18 * lines, 6 * lines)
    vmem = pl.BlockSpec(memory_space=pltpu.VMEM)
    return pl.pallas_call(
        prepare_kernel,
        out_shape=(
            bands,
            bands,
            bands,
            jax.ShapeDtypeStruct(select, jnp.bfloat16),
            jax.ShapeDtypeStruct((2, 256, rows * cols), jnp.bfloat16),
        ),
        in_specs=[vmem] * 3,
        out_specs=(vmem,) * 5,
        scratch_shapes=[pltpu.VMEM((rows * cols // 128, 256, 128), jnp.float32)],
        compiler_params=pltpu.CompilerParams(vmem_limit_bytes=8 << 20),
        cost_estimate=pl.CostEstimate(
            flops=4_000_000, bytes_accessed=4_000_000, transcendentals=0
        ),
    )(x, kernel_one, kernel_two)


def banded_weights(band_ref, group):
    zero = jnp.zeros((CH, 2 * CH), jnp.bfloat16)
    rows = []
    for ab in range(9):
        for i in range(5):
            halves = []
            for m in range(2):
                c = i - 2 * m + 1 - group
                halves.append(band_ref[ab, c] if 0 <= c < 4 else zero)
            rows.append(jnp.concatenate(halves, axis=1))
        if ab % 3 == 2:
            rows.append(jnp.concatenate([zero, zero], axis=1))
    return jnp.concatenate(rows, axis=0)


def gather_depths(plain, turned_lanes):
    zero = jnp.zeros_like(plain[0][0])
    low = lax.broadcasted_iota(jnp.int32, zero.shape, 1) < CH

    def part(tiles, k):
        return tiles[k]

    (p0, p1, p2), (t0, t1, t2) = plain, turned_lanes
    first = [
        part(p0, 0),
        part(p0, 1),
        jnp.where(low, part(p0, 2), part(t1, 0)),
        part(t1, 1),
        part(t1, 2),
        part(p2, 0),
        part(p2, 1),
        jnp.where(low, part(p2, 2), zero),
    ]
    second = [
        part(t0, 2),
        part(t0, 3),
        jnp.where(low, part(t0, 0), part(p1, 1)),
        part(p1, 2),
        part(p1, 3),
        part(t2, 2),
        part(t2, 3),
        jnp.where(low, part(t2, 0), zero),
    ]
    return [jnp.concatenate(half, axis=1).astype(jnp.bfloat16) for half in (first, second)]


def correlate(src, side, band_ref, cols, line, count):
    outs = []
    for group in range(2):
        windows = []
        for a in range(3):
            top = (line + a - 1) * cols
            window = src[group, top : top + count * cols, :]
            if side is not None:
                window = jnp.concatenate([window, side[group, a]], axis=0)
            windows.append(window)
        outs.append(
            jnp.dot(
                jnp.concatenate(windows, axis=1),
                banded_weights(band_ref, group),
                preferred_element_type=jnp.float32,
            )
        )
    return outs


def input_grad_kernel(rows, cols, ps, band_ref, out_ref):
    result = correlate(ps, None, band_ref, cols, 2, rows)
    for group in range(2):
        for r in range(rows):
            out_ref[r, :, 256 * group : 256 * group + 256] = result[group][
                r * cols : r * cols + cols
            ].astype(out_ref.dtype)


def main_kernel(
    rows,
    cols,
    x_ref,
    g_ref,
    ra_ref,
    rb_ref,
    wa_ref,
    wb_ref,
    corner_a_ref,
    corner_b_ref,
    one_ref,
    two_flip_ref,
    select_ref,
    x_t_ref,
    ps,
    *rest,
):
    kg_refs, scratch = rest[:-16], rest[-16:]
    xs, gs, x_side, g_side, sums, acc_one, acc_two, turned_refs = *scratch[:7], scratch[7:9]
    wide_refs, wide_turned_refs = scratch[9:12], scratch[12:15]
    edges_ref = scratch[15]
    f32, bf16 = jnp.float32, jnp.bfloat16
    stride = cols + PAD
    lines = rows + 4
    base = 8
    ha = lax.axis_index("ha")
    wa = lax.axis_index("wa")
    ha_odd = lax.rem(ha, 2)
    wa_odd = lax.rem(wa, 2)

    nothing = lax.shift_right_logical(wa, 16)

    halo = 2 * lines
    gap_rows = (lines + 1) * PAD
    side_rows = 2 * lines

    tiles = x_ref.shape[2] // 128

    def split_lanes(value):
        return [value[:, 128 * k : 128 * k + 128] for k in range(tiles)]

    def turn(parts):
        swapped = [pltpu.roll(part, CH, 1) for part in parts]
        low = lax.broadcasted_iota(jnp.int32, parts[0].shape, 1) < CH
        return [jnp.where(low, swapped[k - 1], swapped[k]) for k in range(tiles)]

    def put_wide(wide, start, count, parts, first=0):
        for k, part in enumerate(parts, first):
            wide[k, pl.ds(start, count), :] = part

    def gather_lines(which, first, last, out):
        wide, wide_turned = wide_refs[which], wide_turned_refs[which]
        top, bottom = base + first * stride, base + last * stride + PAD
        for k, value in enumerate(turn([wide[k, top - 8 : bottom + 8, :] for k in range(tiles)])):
            wide_turned[k, top - 8 : bottom + 8, :] = value
        for l in range(first, last):
            start = base + PAD + l * stride - 1
            where = [start + nothing, start + 1, start + 2 + nothing]
            plain, other = (
                [[ref[k, pl.ds(at, cols), :] for k in range(tiles)] for at in where]
                for ref in (wide, wide_turned)
            )
            for group, value in enumerate(gather_depths(plain, other)):
                out[group, l * cols : (l + 1) * cols, :] = value

    def spread(which, own_ref, out, side_out):
        wide, edges = wide_refs[which], edges_ref.at[which]
        for side, ref in enumerate((wa_ref, wb_ref)):
            pieces = (
                [corner_a_ref[side, which, r] for r in range(2)]
                + [ref[which, r] for r in range(rows)]
                + [corner_b_ref[side, which, r] for r in range(2)]
            )
            for k, piece in enumerate(pieces):
                top = side * halo + 2 * k
                edges[top : top + 2, :] = piece.astype(f32)
        owned = (
            [ra_ref[which, r].astype(f32) for r in range(2)]
            + [own_ref[r].astype(f32) for r in range(rows)]
            + [rb_ref[which, r].astype(f32) for r in range(2)]
        )
        for k, value in enumerate(owned):
            edges[2 * halo + k : 2 * halo + k + 1, :] = value[0:1, :]
            edges[2 * halo + lines + k : 2 * halo + lines + k + 1, :] = value[cols - 1 : cols, :]
        placed = jnp.dot(select_ref[...], edges[...].astype(bf16), preferred_element_type=f32)
        for k in range(lines + 1):
            put_wide(wide, base + k * stride, PAD, split_lanes(placed[k * PAD : (k + 1) * PAD]))
        for r in range(rows):
            start = base + PAD + (r + 2) * stride
            put_wide(wide, start, cols, split_lanes(owned[r + 2]))
        above = base + PAD
        below = base + PAD + (rows + 2) * stride
        a_start = jnp.where(ha_odd == 0, below, above)
        b_start = jnp.where(ha_odd == 0, above, below)
        for r in range(2):
            put_wide(wide, pl.multiple_of(a_start + r * stride, 8), cols, split_lanes(owned[r]))
            put_wide(wide, pl.multiple_of(b_start + r * stride, 8), cols, split_lanes(owned[rows + 2 + r]))
        gather_lines(which, 0, lines, out)
        for a in range(3):
            top = gap_rows + 3 * a * side_rows
            plain = [
                split_lanes(placed[top + b * side_rows : top + (b + 1) * side_rows])
                for b in range(3)
            ]
            other = [turn(parts) for parts in plain]
            for group, value in enumerate(gather_depths(plain, other)):
                side_out[group, a] = value

    count = (rows + 2) * cols
    spread(0, x_ref, xs, x_side)
    pre = correlate(xs, x_side, one_ref, cols, 1, rows + 2)
    spread(1, g_ref, gs, g_side)
    grad_active = correlate(gs, g_side, two_flip_ref, cols, 1, rows + 2)

    ha_last = lax.axis_size("ha") - 1
    wa_last = lax.axis_size("wa") - 1
    position = lax.broadcasted_iota(jnp.int32, (side_rows, 256), 0)
    line = lax.rem(position, lines)
    dead = ((line < 2) & (ha == 0)) | ((line >= rows + 2) & (ha == ha_last))
    dead = dead | ((position < lines) & (wa == 0)) | ((position >= lines) & (wa == wa_last))

    active_t, slopes = [], []
    for group in range(2):
        value = pre[group]
        cdf = 0.5 * (1.0 + lax.erf(value * root_half))
        slopes.append(cdf + value * inv_root_two_pi * jnp.exp(-0.5 * value * value))
        active = (value * cdf)[cols : cols + rows * cols]
        active_t.append(transposed(active, turned_refs[group]))

    half, lead = CH // 2, 8
    low_half = lax.broadcasted_iota(jnp.int32, (CH, 2 * CH), 1) < CH
    low = low_half[:half]

    def kernel_grad(k, fixed, src, acc_ref):
        for a in range(3):
            add_taps(k, a, kernel_grad_parts(fixed, src, acc_ref.at[a], a))

    def kernel_grad_parts(fixed, src, acc_ref, a):
        parts = [[None] * 4 for _ in range(3)]

        def put(window, e, tile):
            old = parts[2 - window][e]
            parts[2 - window][e] = tile if old is None else old + tile

        for group in range(2):
            top = (3 - a) * cols
            acc_ref[...] = jnp.dot(
                fixed[group], src[group, top : top + rows * cols, :], preferred_element_type=f32
            )
            for j in range(4):
                for t in range(8):
                    (window, i), (next_window, next_i) = divmod(2 * t, 5), divmod(2 * t + 1, 5)
                    e = j - i + 1 + group
                    c = j - next_i + 1 + group
                    joined = next_window in (window, 3)
                    use_left = 0 <= e < 4 if joined else 0 <= e < 3
                    use_right = not joined and 0 <= c < 3
                    if not (use_left or use_right):
                        continue
                    tile = acc_ref[64 * j : 64 * j + 64, 128 * t : 128 * t + 128]
                    if use_left:
                        whole = joined or e == 0
                        put(window, e, tile if whole else jnp.where(low_half, tile, 0.0))
                    if use_right:
                        whole = c == 2
                        put(next_window, c + 1, tile if whole else jnp.where(low_half, 0.0, tile))
        return parts

    def add_taps(k, a, parts):
        for b in range(3):
            for c in range(3):
                left, right = parts[b][c], parts[b][c + 1]
                tile = jnp.where(
                    low,
                    left[:half] + pltpu.roll(right[:half], CH, 1),
                    pltpu.roll(left[half:], CH, 1) + right[half:],
                )
                tap = 9 * a + 3 * b + c
                sums[k, lead + half * tap : lead + half * tap + half, :] = tile

    kernel_grad(1, active_t, gs, acc_two)

    edges = edges_ref.at[2]
    for group in range(2):
        lane = slice(256 * group, 256 * group + 256)
        grad_pre = grad_active[group] * slopes[group]
        for l in range(1, rows + 3):
            start = base + PAD + l * stride
            own = grad_pre[(l - 1) * cols : l * cols]
            if l == 1:
                own = jnp.where(ha == 0, 0.0, own)
            if l == rows + 2:
                own = jnp.where(ha == ha_last, 0.0, own)
            put_wide(wide_refs[2], start, cols, [own[:, :128], own[:, 128:]], 2 * group)
        edges[:side_rows, lane] = jnp.where(dead, 0.0, grad_pre[count:])
    for l in range(1, rows + 3):
        left, right = base + l * stride + PAD - 1, base + (l + 1) * stride
        put_wide(wide_refs[2], left, 1, split_lanes(edges[l : l + 1, :]))
        put_wide(wide_refs[2], right, 1, split_lanes(edges[lines + l : lines + l + 1, :]))
    gather_lines(2, 1, rows + 3, ps)

    kernel_grad(0, x_t_ref, ps, acc_one)

    if len(kg_refs) == 1:
        for k in range(2):
            kg_refs[0][k] = sums[k, lead : lead + 27 * half, :]
        return
    keep_ref, send_ref = kg_refs
    slabs, width, share, _ = keep_ref.shape
    take = 27 * half // (2 * slabs * width)
    full, left_over = take // 8 * 8, take % 8
    head = lax.broadcasted_iota(jnp.int32, (8, 2 * CH), 0) < left_over

    def chunk(d):
        at = lead + take * d + nothing
        first = sums[0, pl.ds(at, full + 8), :]
        second = sums[1, pl.ds(at - left_over, share - full), :]
        seam = jnp.where(head, first[full:], second[:8])
        return jnp.concatenate([first[:full], seam, second[8:]], axis=0)

    for z in range(slabs):
        for w in range(width):
            even, odd = (chunk((2 * z + c) * width + w) for c in range(2))
            keep_ref[z, w] = jnp.where(ha_odd == 0, even, odd)
            send_ref[z, w] = jnp.where(ha_odd == 0, odd, even).astype(bf16)


def main(x, g, ra, rb, wa, wb, corner_a, corner_b, one, two_flip, select, x_t, split):
    rows, cols, lanes = x.shape
    stride = cols + PAD
    span = (rows + 4) * stride + PAD
    if split:
        slabs, width = split
        take = 27 * CH // 2 // (2 * slabs * width)
        share = -(-2 * take // 8) * 8
        grads = tuple(
            jax.ShapeDtypeStruct((slabs, width, share, 2 * CH), dtype)
            for dtype in (jnp.float32, jnp.bfloat16)
        )
    else:
        grads = (jax.ShapeDtypeStruct((2, 27 * CH // 2, 2 * CH), jnp.float32),)
    vmem = pl.BlockSpec(memory_space=pltpu.VMEM)
    lines = rows + 4
    moving = (2, lines * cols, 1024)
    side = pltpu.VMEM((2, 3, 2 * lines, 1024), jnp.bfloat16)
    wide = pltpu.VMEM((lanes // 128, span + 16, 128), jnp.float32)
    turning = pltpu.VMEM((rows * cols // 128, 256, 128), jnp.float32)
    return pl.pallas_call(
        functools.partial(main_kernel, rows, cols),
        out_shape=(
            jax.ShapeDtypeStruct(moving, jnp.bfloat16),
            *grads,
        ),
        in_specs=[vmem] * 12,
        out_specs=(vmem,) * (1 + len(grads)),
        scratch_shapes=[
            pltpu.VMEM(moving, jnp.bfloat16),
            pltpu.VMEM(moving, jnp.bfloat16),
            side,
            side,
            pltpu.VMEM((2, 27 * CH // 2 + 40, 2 * CH), jnp.float32),
            pltpu.VMEM((3, 256, 1024), jnp.float32),
            pltpu.VMEM((3, 256, 1024), jnp.float32),
            turning,
            turning,
            *[wide] * 6,
            pltpu.VMEM((3, 6 * lines, lanes), jnp.float32),
        ],
        compiler_params=pltpu.CompilerParams(vmem_limit_bytes=32 << 20),
        cost_estimate=pl.CostEstimate(
            flops=14_000_000_000, bytes_accessed=8_000_000, transcendentals=1_000_000
        ),
    )(x, g, ra, rb, wa, wb, corner_a, corner_b, one, two_flip, select, x_t)


def input_grad(ps, band, shape):
    rows, cols, _ = shape
    vmem = pl.BlockSpec(memory_space=pltpu.VMEM)
    return pl.pallas_call(
        functools.partial(input_grad_kernel, rows, cols),
        out_shape=jax.ShapeDtypeStruct(shape, jnp.bfloat16),
        in_specs=[vmem, vmem],
        out_specs=vmem,
        compiler_params=pltpu.CompilerParams(vmem_limit_bytes=8 << 20),
        cost_estimate=pl.CostEstimate(
            flops=2_000_000_000, bytes_accessed=4_000_000, transcendentals=0
        ),
    )(ps, band)


def xor_exchange(block, axis, mask):
    count = lax.axis_size(axis)
    return lax.ppermute(block, axis, [(i, i ^ mask) for i in range(count)])


def total_of(refs):
    total = refs[0].astype(jnp.float32)
    for ref in refs[1:]:
        total = total + ref.astype(jnp.float32)
    return total


def sum_chip_kernel(keep_ref, got_ref, own_ref, *send_refs):
    wa = lax.axis_index("wa")
    for z in range(keep_ref.shape[0]):
        own_ref[z] = total_of([keep_ref[z, wa], got_ref[z, wa]])
        for k, ref in enumerate(send_refs, 1):
            ref[z] = total_of([keep_ref[z, wa ^ k], got_ref[z, wa ^ k]]).astype(ref.dtype)


def sum_wa_kernel(*refs):
    slabs = refs[0].shape[0]
    got_refs, (own_ref, *send_refs) = refs[:-slabs], refs[-slabs:]
    z = lax.div(lax.axis_index("ha"), 2)
    own_ref[...] = total_of([ref[z] for ref in got_refs])
    for k, ref in enumerate(send_refs, 1):
        ref[...] = total_of([got[z ^ k] for got in got_refs]).astype(ref.dtype)


def sum_z_kernel(*refs):
    total = total_of([ref[...] for ref in refs[:-2]])
    take = refs[-1].shape[0]
    for k, ref in enumerate(refs[-2:]):
        ref[...] = total[k * take : (k + 1) * take]


def reduce_chunks(keep, send, take):
    slabs, width = keep.shape[:2]
    f32, bf16 = jnp.float32, jnp.bfloat16
    unit = keep.shape[2:]
    got = xor_exchange(send, "ha", 1)
    shapes = [jax.ShapeDtypeStruct((slabs,) + unit, f32)]
    shapes += [jax.ShapeDtypeStruct((slabs,) + unit, bf16)] * (width - 1)
    own, *sends = small_call(sum_chip_kernel, tuple(shapes), keep, got)
    got = []
    for k, block in enumerate(sends, 1):
        got.append(xor_exchange(block, "wa", k))
    shapes = [jax.ShapeDtypeStruct(unit, f32)]
    shapes += [jax.ShapeDtypeStruct(unit, f32)] * (slabs - 1)
    own, *sends = small_call(sum_wa_kernel, tuple(shapes), own, *got)
    got = []
    for k, block in enumerate(sends, 1):
        got.append(xor_exchange(block, "ha", 2 * k))
    shapes = (jax.ShapeDtypeStruct((take, 2 * CH), f32),) * 2
    return small_call(sum_z_kernel, shapes, own, *got)


def shards(inputs, grad_out, kernel_one, kernel_two):
    height_count = lax.axis_size("ha")
    width_count = lax.axis_size("wa")
    devices = height_count * width_count
    x, g, kernel_one, kernel_two, to_a, to_b, own_a, own_b = pack(
        inputs, grad_out, kernel_one, kernel_two
    )
    wb = pair_exchange(own_b, "wa", 1)
    wa = pair_exchange(own_a, "wa", 0)
    ra = pair_exchange(to_a, "ha", 0)
    rb = pair_exchange(to_b, "ha", 1)
    one, two_flip, one_flip, select, x_t = prepare(x, kernel_one, kernel_two)
    corner_to_a, corner_to_b = corners(wa, wb)
    corner_b = pair_exchange(corner_to_b, "ha", 1)
    corner_a = pair_exchange(corner_to_a, "ha", 0)

    split = None
    if (
        (27 * CH // 2) % devices == 0
        and height_count & (height_count - 1) == 0
        and width_count & (width_count - 1) == 0
        and height_count > 1
    ):
        split = (height_count // 2, width_count)
    ps, *grads = main(x, g, ra, rb, wa, wb, corner_a, corner_b, one, two_flip, select, x_t, split)
    grad_inputs = input_grad(ps, one_flip, inputs.shape)
    if split:
        grads = reduce_chunks(*grads, 27 * CH // 2 // devices)
    else:
        grads = [
            lax.psum_scatter(
                grads[0][k].reshape(devices, -1), ("ha", "wa"), scatter_dimension=0, tiled=True
            )
            for k in range(2)
        ]
    return (grad_inputs, grads[0].reshape(-1), grads[1].reshape(-1))


def solution(mesh):
    return jax.shard_map(
        shards,
        mesh=mesh,
        in_specs=(P("ha", "wa", None), P("ha", "wa", None), P(), P()),
        out_specs=(P("ha", "wa", None), P(("ha", "wa")), P(("ha", "wa"))),
        check_vma=False,
    )
```

```python
import functools

import jax
import jax.numpy as jnp
from jax import lax
from jax.experimental import pallas as pl
from jax.experimental.pallas import tpu as pltpu
from jax.sharding import PartitionSpec as P


CH = 64
PAD = 16

root_half = 0.7071067811865476
inv_root_two_pi = 0.3989422804014327


def pair_exchange(block, axis, first):
    count = lax.axis_size(axis)
    pairs = []
    for low in range(first, count - 1, 2):
        pairs += [(low, low + 1), (low + 1, low)]
    return lax.ppermute(block, axis, pairs)


def in_hbm(block):
    return pltpu.with_memory_space_constraint(block, pltpu.HBM)


def pack_kernel(
    x_hbm, g_hbm, one_hbm, two_hbm, x_ref, g_ref, one_ref, two_ref, to_a, to_b, own_a, own_b, sems
):
    rows, cols, _ = x_ref.shape
    pairs = ((x_hbm, x_ref), (g_hbm, g_ref), (one_hbm, one_ref), (two_hbm, two_ref))
    copies = [
        pltpu.make_async_copy(source, target, sems.at[k])
        for k, (source, target) in enumerate(pairs)
    ]
    for copy in copies:
        copy.start()
    ha_even = lax.rem(lax.axis_index("ha"), 2) == 0
    wa_even = lax.rem(lax.axis_index("wa"), 2) == 0
    a_start = jnp.where(ha_even, rows - 2, 0)
    b_start = jnp.where(ha_even, 0, rows - 2)
    for which, ref in enumerate((x_ref, g_ref)):
        copies[which].wait()
        to_a[which] = ref[pl.ds(a_start, 2)]
        to_b[which] = ref[pl.ds(b_start, 2)]
        for r in range(rows):
            left, right = ref[r, 0:2, :], ref[r, cols - 2 : cols, :]
            own_a[which, r] = jnp.where(wa_even, right, left)
            own_b[which, r] = jnp.where(wa_even, left, right)
    for copy in copies[2:]:
        copy.wait()


def pack(x, g, one, two):
    rows, cols, lanes = x.shape
    vmem = pl.BlockSpec(memory_space=pltpu.VMEM)
    hbm = pl.BlockSpec(memory_space=pltpu.HBM)
    shapes = [x.shape] * 2 + [one.shape] * 2
    shapes += [(2, 2, cols, lanes)] * 2 + [(2, rows, 2, lanes)] * 2
    return pl.pallas_call(
        pack_kernel,
        out_shape=tuple(jax.ShapeDtypeStruct(shape, x.dtype) for shape in shapes),
        in_specs=[hbm] * 4,
        out_specs=(vmem,) * 8,
        scratch_shapes=[pltpu.SemaphoreType.DMA((4,))],
        compiler_params=pltpu.CompilerParams(vmem_limit_bytes=4 << 20),
        cost_estimate=pl.CostEstimate(flops=0, bytes_accessed=1_100_000, transcendentals=0),
    )(*(in_hbm(block) for block in (x, g, one, two)))


def corners_kernel(wa_ref, wb_ref, to_a, to_b):
    rows = wa_ref.shape[1]
    ha_even = lax.rem(lax.axis_index("ha"), 2) == 0
    a_start = jnp.where(ha_even, rows - 2, 0)
    b_start = jnp.where(ha_even, 0, rows - 2)
    for side, ref in enumerate((wa_ref, wb_ref)):
        for which in range(2):
            for r in range(2):
                to_a[side, which, r] = ref[which, a_start + r]
                to_b[side, which, r] = ref[which, b_start + r]


def small_call(kernel, out_shape, *operands):
    vmem = pl.BlockSpec(memory_space=pltpu.VMEM)
    return pl.pallas_call(
        kernel,
        out_shape=out_shape,
        in_specs=[vmem] * len(operands),
        out_specs=(vmem,) * len(out_shape),
        compiler_params=pltpu.CompilerParams(vmem_limit_bytes=2 << 20),
        cost_estimate=pl.CostEstimate(flops=0, bytes_accessed=300_000, transcendentals=0),
    )(*operands)


def corners(wa, wb):
    shape = jax.ShapeDtypeStruct((2, 2, 2) + wa.shape[2:], wa.dtype)
    return small_call(corners_kernel, (shape, shape), wa, wb)


def halo_selection(lines, shape):
    ha_odd = lax.rem(lax.axis_index("ha"), 2)
    wa_odd = lax.rem(lax.axis_index("wa"), 2)
    halo = 2 * lines
    gap_rows = (lines + 1) * PAD
    side_rows = 2 * lines
    q = lax.broadcasted_iota(jnp.int32, shape, 0)
    col = lax.broadcasted_iota(jnp.int32, shape, 1)

    def order(line):
        swapped = jnp.where(
            line < 2, line + lines - 2, jnp.where(line >= lines - 2, line - lines + 2, line)
        )
        return jnp.where(ha_odd == 0, swapped, line)

    left_base = jnp.where(wa_odd == 0, halo, 0)
    right_base = jnp.where(wa_odd == 0, 0, halo)
    gap = lax.div(q, PAD)
    w = lax.rem(q, PAD)
    left_hit = (w == PAD - 1) & (gap < lines) & (col == left_base + 2 * order(gap) + 1)
    right_hit = (w == 0) & (gap >= 1) & (col == right_base + 2 * order(gap - 1))
    in_gaps = (q < gap_rows) & (left_hit | right_hit)
    q = q - gap_rows
    tap = lax.div(q, side_rows)
    b = lax.rem(tap, 3)
    right = lax.div(lax.rem(q, side_rows), lines)
    line = lax.rem(q, lines) + lax.div(tap, 3) - 1
    at = order(line)
    left_source = jnp.where(b == 2, 2 * halo + at, left_base + 2 * at + b)
    right_source = jnp.where(b == 0, 2 * halo + lines + at, right_base + 2 * at + b - 1)
    source = jnp.where(right == 0, left_source, right_source)
    in_sides = (q >= 0) & (line >= 0) & (line < lines) & (col == source)
    return jnp.where(in_gaps | in_sides, 1.0, 0.0).astype(jnp.bfloat16)


def transposed(value, turned):
    flat = jnp.transpose(value)
    halves = []
    for side in range(flat.shape[1] // 128):
        turned[side] = flat[:, 128 * side : 128 * side + 128]
        pieces = [
            turned[side, pl.ds(64 * j + odd, 32, stride=2), :] for j in range(4) for odd in range(2)
        ]
        halves.append(jnp.concatenate(pieces, axis=0))
    return jnp.concatenate(halves, axis=1).astype(jnp.bfloat16)


def prepare_kernel(
    lines, one_ref, two_ref, one_out, two_flip_out, one_flip_out, select_out
):
    select_out[...] = halo_selection(lines, select_out.shape)
    zero = jnp.zeros((CH, CH), jnp.bfloat16)

    def banded(tiles):
        padded = [zero] + tiles + [zero]
        return [jnp.concatenate([padded[c + 1], padded[c]], axis=1) for c in range(4)]

    def flipped(ref, tap):
        return jnp.transpose(ref[26 - tap].astype(jnp.float32)).astype(jnp.bfloat16)

    for ab in range(9):
        taps = [3 * ab + c for c in range(3)]
        for c, tile in enumerate(banded([one_ref[t] for t in taps])):
            one_out[ab, c] = tile
        for c, tile in enumerate(banded([flipped(two_ref, t) for t in taps])):
            two_flip_out[ab, c] = tile
        for c, tile in enumerate(banded([flipped(one_ref, t) for t in taps])):
            one_flip_out[ab, c] = tile


def prepare(lines, kernel_one, kernel_two):
    bands = jax.ShapeDtypeStruct((9, 4, CH, 2 * CH), jnp.bfloat16)
    select = ((lines + 1) * PAD + 18 * lines, 6 * lines)
    vmem = pl.BlockSpec(memory_space=pltpu.VMEM)
    return pl.pallas_call(
        functools.partial(prepare_kernel, lines),
        out_shape=(bands, bands, bands, jax.ShapeDtypeStruct(select, jnp.bfloat16)),
        in_specs=[vmem] * 2,
        out_specs=(vmem,) * 4,
        compiler_params=pltpu.CompilerParams(vmem_limit_bytes=8 << 20),
        cost_estimate=pl.CostEstimate(
            flops=4_000_000, bytes_accessed=4_000_000, transcendentals=0
        ),
    )(kernel_one, kernel_two)


def banded_weights(band_ref, group):
    zero = jnp.zeros((CH, 2 * CH), jnp.bfloat16)
    rows = []
    for ab in range(9):
        for i in range(5):
            halves = []
            for m in range(2):
                c = i - 2 * m + 1 - group
                halves.append(band_ref[ab, c] if 0 <= c < 4 else zero)
            rows.append(jnp.concatenate(halves, axis=1))
        if ab % 3 == 2:
            rows.append(jnp.concatenate([zero, zero], axis=1))
    return jnp.concatenate(rows, axis=0)


def gather_depths(plain, turned_lanes):
    zero = jnp.zeros_like(plain[0][0])
    low = lax.broadcasted_iota(jnp.int32, zero.shape, 1) < CH

    def part(tiles, k):
        return tiles[k]

    (p0, p1, p2), (t0, t1, t2) = plain, turned_lanes
    first = [
        part(p0, 0),
        part(p0, 1),
        jnp.where(low, part(p0, 2), part(t1, 0)),
        part(t1, 1),
        part(t1, 2),
        part(p2, 0),
        part(p2, 1),
        jnp.where(low, part(p2, 2), zero),
    ]
    second = [
        part(t0, 2),
        part(t0, 3),
        jnp.where(low, part(t0, 0), part(p1, 1)),
        part(p1, 2),
        part(p1, 3),
        part(t2, 2),
        part(t2, 3),
        jnp.where(low, part(t2, 0), zero),
    ]
    return [jnp.concatenate(half, axis=1).astype(jnp.bfloat16) for half in (first, second)]


def correlate(src, side, band_ref, cols, runs):
    outs = []
    for group in range(2):
        windows = []
        for a in range(3):
            parts = [
                src[group, (line + a - 1) * cols : (line + a - 1 + count) * cols, :]
                for line, count in runs
            ]
            if side is not None:
                parts.append(side[group, a])
            windows.append(parts[0] if len(parts) == 1 else jnp.concatenate(parts, axis=0))
        outs.append(
            jnp.dot(
                jnp.concatenate(windows, axis=1),
                banded_weights(band_ref, group),
                preferred_element_type=jnp.float32,
            )
        )
    return outs


def input_grad_kernel(rows, cols, ps, band_ref, out_ref):
    result = correlate(ps, None, band_ref, cols, [(2, rows)])
    for group in range(2):
        for r in range(rows):
            out_ref[r, :, 256 * group : 256 * group + 256] = result[group][
                r * cols : r * cols + cols
            ].astype(out_ref.dtype)


def field_tools(
    rows, cols, ra_ref, rb_ref, wa_ref, wb_ref, corner_a_ref, corner_b_ref, select_ref, scratch
):
    wide_refs, wide_turned_refs, edges_ref = scratch
    f32, bf16 = jnp.float32, jnp.bfloat16
    stride = cols + PAD
    lines = rows + 4
    base = 8
    ha = lax.axis_index("ha")
    wa = lax.axis_index("wa")
    ha_odd = lax.rem(ha, 2)
    wa_odd = lax.rem(wa, 2)

    nothing = lax.shift_right_logical(wa, 16)

    halo = 2 * lines
    gap_rows = (lines + 1) * PAD
    side_rows = 2 * lines

    tiles = ra_ref.shape[3] // 128

    def split_lanes(value):
        return [value[:, 128 * k : 128 * k + 128] for k in range(tiles)]

    def turn(parts):
        swapped = [pltpu.roll(part, CH, 1) for part in parts]
        low = lax.broadcasted_iota(jnp.int32, parts[0].shape, 1) < CH
        return [jnp.where(low, swapped[k - 1], swapped[k]) for k in range(tiles)]

    def put_wide(wide, start, count, parts, first=0):
        for k, part in enumerate(parts, first):
            wide[k, pl.ds(start, count), :] = part

    def gather_lines(which, first, last, out):
        wide, wide_turned = wide_refs[which], wide_turned_refs[which]
        top, bottom = base + first * stride, base + last * stride + PAD
        for k, value in enumerate(turn([wide[k, top - 8 : bottom + 8, :] for k in range(tiles)])):
            wide_turned[k, top - 8 : bottom + 8, :] = value
        for l in range(first, last):
            start = base + PAD + l * stride - 1
            where = [start + nothing, start + 1, start + 2 + nothing]
            plain, other = (
                [[ref[k, pl.ds(at, cols), :] for k in range(tiles)] for at in where]
                for ref in (wide, wide_turned)
            )
            for group, value in enumerate(gather_depths(plain, other)):
                out[group, l * cols : (l + 1) * cols, :] = value

    def spread(which, own_ref, out, side_out, gathered):
        wide, edges = wide_refs[which], edges_ref.at[which]
        for side, ref in enumerate((wa_ref, wb_ref)):
            pieces = (
                [corner_a_ref[side, which, r] for r in range(2)]
                + [ref[which, r] for r in range(rows)]
                + [corner_b_ref[side, which, r] for r in range(2)]
            )
            for k, piece in enumerate(pieces):
                top = side * halo + 2 * k
                edges[top : top + 2, :] = piece.astype(f32)
        owned = (
            [ra_ref[which, r].astype(f32) for r in range(2)]
            + [own_ref[r].astype(f32) for r in range(rows)]
            + [rb_ref[which, r].astype(f32) for r in range(2)]
        )
        for k, value in enumerate(owned):
            edges[2 * halo + k : 2 * halo + k + 1, :] = value[0:1, :]
            edges[2 * halo + lines + k : 2 * halo + lines + k + 1, :] = value[cols - 1 : cols, :]
        used = gap_rows if side_out is None else select_ref.shape[0]
        placed = jnp.dot(select_ref[:used], edges[...].astype(bf16), preferred_element_type=f32)
        for k in range(lines + 1):
            put_wide(wide, base + k * stride, PAD, split_lanes(placed[k * PAD : (k + 1) * PAD]))
        for r in range(rows):
            start = base + PAD + (r + 2) * stride
            put_wide(wide, start, cols, split_lanes(owned[r + 2]))
        above = base + PAD
        below = base + PAD + (rows + 2) * stride
        a_start = jnp.where(ha_odd == 0, below, above)
        b_start = jnp.where(ha_odd == 0, above, below)
        for r in range(2):
            put_wide(wide, pl.multiple_of(a_start + r * stride, 8), cols, split_lanes(owned[r]))
            put_wide(wide, pl.multiple_of(b_start + r * stride, 8), cols, split_lanes(owned[rows + 2 + r]))
        for first, last in gathered:
            gather_lines(which, first, last, out)
        for a in range(0 if side_out is None else 3):
            top = gap_rows + 3 * a * side_rows
            plain = [
                split_lanes(placed[top + b * side_rows : top + (b + 1) * side_rows])
                for b in range(3)
            ]
            other = [turn(parts) for parts in plain]
            for group, value in enumerate(gather_depths(plain, other)):
                side_out[group, a] = value

    return spread, gather_lines, put_wide, split_lanes


def main_kernel(
    rows,
    cols,
    x_ref,
    g_ref,
    ra_ref,
    rb_ref,
    wa_ref,
    wb_ref,
    corner_a_ref,
    corner_b_ref,
    select_ref,
    one_ref,
    two_flip_ref,
    grad_pre_ref,
    *rest,
):
    f32, bf16 = jnp.float32, jnp.bfloat16
    kg_refs, scratch = rest[:-13], rest[-13:]
    xs, gs, sums, acc_one, acc_two, turned_refs = *scratch[:5], scratch[5:7]
    swap = scratch[7]
    spread, _, _, _ = field_tools(
        rows,
        cols,
        ra_ref,
        rb_ref,
        wa_ref,
        wb_ref,
        corner_a_ref,
        corner_b_ref,
        select_ref,
        (scratch[8:10], scratch[10:12], scratch[12]),
    )
    lines = rows + 4
    ha_odd = lax.rem(lax.axis_index("ha"), 2)
    nothing = lax.shift_right_logical(lax.axis_index("wa"), 16)

    spread(0, x_ref, xs, None, [(1, lines - 1)])
    pre = correlate(xs, None, one_ref, cols, [(2, rows)])
    spread(1, g_ref, gs, None, [(1, lines - 1)])
    grad_active = correlate(gs, None, two_flip_ref, cols, [(2, rows)])

    active_t, slopes = [], []
    for group in range(2):
        value = pre[group]
        cdf = 0.5 * (1.0 + lax.erf(value * root_half))
        slopes.append(cdf + value * inv_root_two_pi * jnp.exp(-0.5 * value * value))
        active_t.append(transposed(value * cdf, turned_refs[group]))

    half, lead = CH // 2, 8
    low_half = lax.broadcasted_iota(jnp.int32, (CH, 2 * CH), 1) < CH
    low = low_half[:half]

    def kernel_grad_parts(fixed, src, acc_ref, a):
        parts = [[None] * 4 for _ in range(3)]

        def put(window, e, tile):
            old = parts[2 - window][e]
            parts[2 - window][e] = tile if old is None else old + tile

        for group in range(2):
            top = (3 - a) * cols
            acc_ref[...] = jnp.dot(
                fixed[group], src[group, top : top + rows * cols, :], preferred_element_type=f32
            )
            for j in range(4):
                for t in range(8):
                    (window, i), (next_window, next_i) = divmod(2 * t, 5), divmod(2 * t + 1, 5)
                    e = j - i + 1 + group
                    c = j - next_i + 1 + group
                    joined = next_window in (window, 3)
                    use_left = 0 <= e < 4 if joined else 0 <= e < 3
                    use_right = not joined and 0 <= c < 3
                    if not (use_left or use_right):
                        continue
                    tile = acc_ref[64 * j : 64 * j + 64, 128 * t : 128 * t + 128]
                    if use_left:
                        whole = joined or e == 0
                        put(window, e, tile if whole else jnp.where(low_half, tile, 0.0))
                    if use_right:
                        whole = c == 2
                        put(next_window, c + 1, tile if whole else jnp.where(low_half, 0.0, tile))
        return parts

    def put_tile(k, tap, left, right):
        sums[k, lead + half * tap : lead + half * tap + half, :] = jnp.where(low, left, right)

    def add_taps(a, parts):
        for b in range(3):
            for c in range(3):
                left, right = parts[b][c], parts[b][c + 1]
                put_tile(
                    1,
                    9 * a + 3 * b + c,
                    left[:half] + pltpu.roll(right[:half], CH, 1),
                    pltpu.roll(left[half:], CH, 1) + right[half:],
                )

    def first_grad(fixed, src, a):
        parts = [[None] * 4 for _ in range(3)]

        def put(window, e, tile):
            old = parts[window][e + 1]
            parts[window][e + 1] = tile if old is None else old + tile

        for group in range(2):
            top = (a + 1) * cols
            acc_ref = acc_one.at[2 * a + group]
            acc_ref[...] = jnp.dot(
                fixed[group], src[group, top : top + rows * cols, :], preferred_element_type=f32
            )
            for j in range(4):
                for t in range(8):
                    (window, i), (next_window, next_i) = divmod(2 * t, 5), divmod(2 * t + 1, 5)
                    e = i - j + 1 - group
                    c = next_i - j + 1 - group
                    joined = next_window in (window, 3)
                    use_left = -1 <= e < 3 if joined else 0 <= e < 3
                    use_right = not joined and 0 <= c < 3
                    if not (use_left or use_right):
                        continue
                    tile = acc_ref[64 * j : 64 * j + 64, 128 * t : 128 * t + 128]
                    if use_left:
                        whole = joined or e == 2
                        put(window, e, tile if whole else jnp.where(low_half, tile, 0.0))
                    if use_right:
                        whole = c == 0
                        put(next_window, c - 1, tile if whole else jnp.where(low_half, 0.0, tile))

        def joined_halves(b, c, d):
            first = parts[b][c + 1] + pltpu.roll(parts[b][c], CH, 1)
            second = pltpu.roll(parts[b][d + 1], CH, 1) + parts[b][d]
            return jnp.where(low_half, first, second)

        for b in range(3):
            for k, (c, d) in enumerate(((0, 1), (2, 2))):
                slot = swap.at[2 * (3 * a + b) + k]
                slot[:, :CH] = jnp.transpose(joined_halves(b, c, d))
                for tap, at in ((c, 0), (d, CH))[: 1 + (c != d)]:
                    even = slot[pl.ds(at, half, stride=2), :]
                    odd = slot[pl.ds(at + 1, half, stride=2), :]
                    put_tile(0, 9 * a + 3 * b + tap, even, pltpu.roll(odd, CH, 1))

    for a in range(2):
        add_taps(a, kernel_grad_parts(active_t, gs, acc_two.at[a], a))
    grad_pre_t = []
    for group in range(2):
        grad_pre = grad_active[group] * slopes[group]
        grad_pre_ref[:, 256 * group : 256 * group + 256] = grad_pre.astype(bf16)
        grad_pre_t.append(jnp.transpose(grad_pre).astype(bf16))
    for a in range(3):
        first_grad(grad_pre_t, xs, a)
    add_taps(2, kernel_grad_parts(active_t, gs, acc_two.at[2], 2))

    if len(kg_refs) == 1:
        for k in range(2):
            kg_refs[0][k] = sums[k, lead : lead + 27 * half, :]
        return
    keep_ref, send_ref = kg_refs
    slabs, width, share, _ = keep_ref.shape
    take = 27 * half // (2 * slabs * width)
    full, left_over = take // 8 * 8, take % 8
    head = lax.broadcasted_iota(jnp.int32, (8, 2 * CH), 0) < left_over

    def chunk(d):
        at = lead + take * d + nothing
        first = sums[0, pl.ds(at, full + 8), :]
        second = sums[1, pl.ds(at - left_over, share - full), :]
        seam = jnp.where(head, first[full:], second[:8])
        return jnp.concatenate([first[:full], seam, second[8:]], axis=0)

    for z in range(slabs):
        for w in range(width):
            even, odd = (chunk((2 * z + c) * width + w) for c in range(2))
            keep_ref[z, w] = jnp.where(ha_odd == 0, even, odd)
            send_ref[z, w] = jnp.where(ha_odd == 0, odd, even).astype(bf16)


def ring_kernel(
    rows,
    cols,
    x_ref,
    g_ref,
    ra_ref,
    rb_ref,
    wa_ref,
    wb_ref,
    corner_a_ref,
    corner_b_ref,
    select_ref,
    one_ref,
    two_flip_ref,
    grad_pre_ref,
    ps,
    *scratch,
):
    f32 = jnp.float32
    xs, gs, x_side, g_side = scratch[:4]
    wide_refs, edges_ref = scratch[4:7], scratch[10]
    spread, gather_lines, put_wide, split_lanes = field_tools(
        rows,
        cols,
        ra_ref,
        rb_ref,
        wa_ref,
        wb_ref,
        corner_a_ref,
        corner_b_ref,
        select_ref,
        (wide_refs, scratch[7:10], edges_ref),
    )
    lines, stride, base = rows + 4, cols + PAD, 8
    side_rows = 2 * lines
    ha, wa = lax.axis_index("ha"), lax.axis_index("wa")
    ha_last = lax.axis_size("ha") - 1
    wa_last = lax.axis_size("wa") - 1
    runs = [(1, 1), (rows + 2, 1)]
    gathered = [(0, 3), (lines - 3, lines)]
    spread(0, x_ref, xs, x_side, gathered)
    pre = correlate(xs, x_side, one_ref, cols, runs)
    spread(1, g_ref, gs, g_side, gathered)
    grad_active = correlate(gs, g_side, two_flip_ref, cols, runs)
    position = lax.broadcasted_iota(jnp.int32, (side_rows, 256), 0)
    line = lax.rem(position, lines)
    dead = ((line < 2) & (ha == 0)) | ((line >= rows + 2) & (ha == ha_last))
    dead = dead | ((position < lines) & (wa == 0)) | ((position >= lines) & (wa == wa_last))
    wide, edges = wide_refs[2], edges_ref.at[2]
    for r in range(rows):
        own = grad_pre_ref[r * cols : r * cols + cols, :].astype(f32)
        put_wide(wide, base + PAD + (r + 2) * stride, cols, split_lanes(own))
    for group in range(2):
        value = pre[group]
        cdf = 0.5 * (1.0 + lax.erf(value * root_half))
        slope = cdf + value * inv_root_two_pi * jnp.exp(-0.5 * value * value)
        grad_pre = grad_active[group] * slope
        above = jnp.where(ha == 0, 0.0, grad_pre[:cols])
        below = jnp.where(ha == ha_last, 0.0, grad_pre[cols : 2 * cols])
        for l, part in ((1, above), (rows + 2, below)):
            start = base + PAD + l * stride
            put_wide(wide, start, cols, [part[:, :128], part[:, 128:]], 2 * group)
        edges[:side_rows, 256 * group : 256 * group + 256] = jnp.where(
            dead, 0.0, grad_pre[2 * cols :]
        )
    for l in range(1, rows + 3):
        left, right = base + l * stride + PAD - 1, base + (l + 1) * stride
        put_wide(wide, left, 1, split_lanes(edges[l : l + 1, :]))
        put_wide(wide, right, 1, split_lanes(edges[lines + l : lines + l + 1, :]))
    gather_lines(2, 1, rows + 3, ps)


def scratch_shapes(rows, cols, lanes, fields):
    span = (rows + 4) * (cols + PAD) + PAD
    wide = pltpu.VMEM((lanes // 128, span + 16, 128), jnp.float32)
    return [*[wide] * (2 * fields), pltpu.VMEM((fields, 6 * (rows + 4), lanes), jnp.float32)]


def main(fields, bands, split):
    rows, cols, lanes = fields[0].shape
    if split:
        slabs, width = split
        take = 27 * CH // 2 // (2 * slabs * width)
        share = -(-2 * take // 8) * 8
        grads = tuple(
            jax.ShapeDtypeStruct((slabs, width, share, 2 * CH), dtype)
            for dtype in (jnp.float32, jnp.bfloat16)
        )
    else:
        grads = (jax.ShapeDtypeStruct((2, 27 * CH // 2, 2 * CH), jnp.float32),)
    vmem = pl.BlockSpec(memory_space=pltpu.VMEM)
    moving = pltpu.VMEM((2, (rows + 4) * cols, 1024), jnp.bfloat16)
    turning = pltpu.VMEM((rows * cols // 128, 256, 128), jnp.float32)
    return pl.pallas_call(
        functools.partial(main_kernel, rows, cols),
        out_shape=(jax.ShapeDtypeStruct((rows * cols, lanes), jnp.bfloat16), *grads),
        in_specs=[vmem] * 11,
        out_specs=(vmem,) * (1 + len(grads)),
        scratch_shapes=[
            moving,
            moving,
            pltpu.VMEM((2, 27 * CH // 2 + 40, 2 * CH), jnp.float32),
            pltpu.VMEM((6, 256, 1024), jnp.float32),
            pltpu.VMEM((3, 256, 1024), jnp.float32),
            turning,
            turning,
            pltpu.VMEM((18, 2 * CH, 2 * CH), jnp.float32),
            *scratch_shapes(rows, cols, lanes, 2),
        ],
        compiler_params=pltpu.CompilerParams(vmem_limit_bytes=32 << 20),
        cost_estimate=pl.CostEstimate(
            flops=10_000_000_000, bytes_accessed=8_000_000, transcendentals=1_000_000
        ),
    )(*fields, *bands)


def ring(fields, bands, grad_pre):
    rows, cols, lanes = fields[0].shape
    vmem = pl.BlockSpec(memory_space=pltpu.VMEM)
    moving = ((2, (rows + 4) * cols, 1024), jnp.bfloat16)
    side = pltpu.VMEM((2, 3, 2 * (rows + 4), 1024), jnp.bfloat16)
    return pl.pallas_call(
        functools.partial(ring_kernel, rows, cols),
        out_shape=jax.ShapeDtypeStruct(*moving),
        in_specs=[vmem] * 12,
        out_specs=vmem,
        scratch_shapes=[
            pltpu.VMEM(*moving),
            pltpu.VMEM(*moving),
            side,
            side,
            *scratch_shapes(rows, cols, lanes, 3),
        ],
        compiler_params=pltpu.CompilerParams(vmem_limit_bytes=20 << 20),
        cost_estimate=pl.CostEstimate(
            flops=3_000_000_000, bytes_accessed=8_000_000, transcendentals=500_000
        ),
    )(*fields, *bands, grad_pre)


def input_grad(ps, band, shape):
    rows, cols, _ = shape
    vmem = pl.BlockSpec(memory_space=pltpu.VMEM)
    return pl.pallas_call(
        functools.partial(input_grad_kernel, rows, cols),
        out_shape=jax.ShapeDtypeStruct(shape, jnp.bfloat16),
        in_specs=[vmem, vmem],
        out_specs=vmem,
        compiler_params=pltpu.CompilerParams(vmem_limit_bytes=8 << 20),
        cost_estimate=pl.CostEstimate(
            flops=2_000_000_000, bytes_accessed=4_000_000, transcendentals=0
        ),
    )(ps, band)


def xor_exchange(block, axis, mask):
    count = lax.axis_size(axis)
    return lax.ppermute(block, axis, [(i, i ^ mask) for i in range(count)])


def total_of(refs):
    total = refs[0].astype(jnp.float32)
    for ref in refs[1:]:
        total = total + ref.astype(jnp.float32)
    return total


def sum_chip_kernel(keep_ref, got_ref, own_ref, *send_refs):
    wa = lax.axis_index("wa")
    for z in range(keep_ref.shape[0]):
        own_ref[z] = total_of([keep_ref[z, wa], got_ref[z, wa]])
        for k, ref in enumerate(send_refs, 1):
            ref[z] = total_of([keep_ref[z, wa ^ k], got_ref[z, wa ^ k]]).astype(ref.dtype)


def sum_wa_kernel(*refs):
    slabs = refs[0].shape[0]
    got_refs, (own_ref, *send_refs) = refs[:-slabs], refs[-slabs:]
    z = lax.div(lax.axis_index("ha"), 2)
    own_ref[...] = total_of([ref[z] for ref in got_refs])
    for k, ref in enumerate(send_refs, 1):
        ref[...] = total_of([got[z ^ k] for got in got_refs]).astype(ref.dtype)


def sum_z_kernel(*refs):
    total = total_of([ref[...] for ref in refs[:-2]])
    take = refs[-1].shape[0]
    for k, ref in enumerate(refs[-2:]):
        ref[...] = total[k * take : (k + 1) * take]


def reduce_chunks(keep, send, take):
    slabs, width = keep.shape[:2]
    f32, bf16 = jnp.float32, jnp.bfloat16
    unit = keep.shape[2:]
    got = xor_exchange(send, "ha", 1)
    shapes = [jax.ShapeDtypeStruct((slabs,) + unit, f32)]
    shapes += [jax.ShapeDtypeStruct((slabs,) + unit, bf16)] * (width - 1)
    own, *sends = small_call(sum_chip_kernel, tuple(shapes), keep, got)
    got = []
    for k, block in enumerate(sends, 1):
        got.append(xor_exchange(block, "wa", k))
    shapes = [jax.ShapeDtypeStruct(unit, f32)]
    shapes += [jax.ShapeDtypeStruct(unit, f32)] * (slabs - 1)
    own, *sends = small_call(sum_wa_kernel, tuple(shapes), own, *got)
    got = []
    for k, block in enumerate(sends, 1):
        got.append(xor_exchange(block, "ha", 2 * k))
    shapes = (jax.ShapeDtypeStruct((take, 2 * CH), f32),) * 2
    return small_call(sum_z_kernel, shapes, own, *got)


def shards(inputs, grad_out, kernel_one, kernel_two):
    rows, _, _ = inputs.shape
    height_count = lax.axis_size("ha")
    width_count = lax.axis_size("wa")
    devices = height_count * width_count
    x, g, kernel_one, kernel_two, to_a, to_b, own_a, own_b = pack(
        inputs, grad_out, kernel_one, kernel_two
    )
    wb = pair_exchange(own_b, "wa", 1)
    wa = pair_exchange(own_a, "wa", 0)
    ra = pair_exchange(to_a, "ha", 0)
    rb = pair_exchange(to_b, "ha", 1)
    one, two_flip, one_flip, select = prepare(rows + 4, kernel_one, kernel_two)
    corner_to_a, corner_to_b = corners(wa, wb)
    corner_b = pair_exchange(corner_to_b, "ha", 1)
    corner_a = pair_exchange(corner_to_a, "ha", 0)

    split = None
    if (
        (27 * CH // 2) % devices == 0
        and height_count & (height_count - 1) == 0
        and width_count & (width_count - 1) == 0
        and height_count > 1
    ):
        split = (height_count // 2, width_count)
    fields = (x, g, ra, rb, wa, wb, corner_a, corner_b)
    bands = (select, one, two_flip)
    grad_pre, *grads = main(fields, bands, split)
    ps = ring(fields, bands, grad_pre)
    grad_inputs = input_grad(ps, one_flip, inputs.shape)
    if split:
        grads = reduce_chunks(*grads, 27 * CH // 2 // devices)
    else:
        grads = [
            lax.psum_scatter(
                grads[0][k].reshape(devices, -1), ("ha", "wa"), scatter_dimension=0, tiled=True
            )
            for k in range(2)
        ]
    return (grad_inputs, grads[0].reshape(-1), grads[1].reshape(-1))


def solution(mesh):
    return jax.shard_map(
        shards,
        mesh=mesh,
        in_specs=(P("ha", "wa", None), P("ha", "wa", None), P(), P()),
        out_specs=(P("ha", "wa", None), P(("ha", "wa")), P(("ha", "wa"))),
        check_vma=False,
    )
```

```python
import functools

import jax
import jax.numpy as jnp
from jax import lax
from jax.experimental import pallas as pl
from jax.experimental.pallas import tpu as pltpu
from jax.sharding import PartitionSpec as P


CH = 64
PAD = 16

root_half = 0.7071067811865476
inv_root_two_pi = 0.3989422804014327


def pair_exchange(block, axis, first):
    count = lax.axis_size(axis)
    pairs = []
    for low in range(first, count - 1, 2):
        pairs += [(low, low + 1), (low + 1, low)]
    return lax.ppermute(block, axis, pairs)


def in_hbm(block):
    return pltpu.with_memory_space_constraint(block, pltpu.HBM)


def pack_kernel(
    x_hbm, g_hbm, one_hbm, two_hbm, x_ref, g_ref, one_ref, two_ref, to_a, to_b, own_a, own_b, sems
):
    rows, cols, _ = x_ref.shape
    pairs = ((x_hbm, x_ref), (g_hbm, g_ref), (one_hbm, one_ref), (two_hbm, two_ref))
    copies = [
        pltpu.make_async_copy(source, target, sems.at[k])
        for k, (source, target) in enumerate(pairs)
    ]
    for copy in copies:
        copy.start()
    ha_even = lax.rem(lax.axis_index("ha"), 2) == 0
    wa_even = lax.rem(lax.axis_index("wa"), 2) == 0
    a_start = jnp.where(ha_even, rows - 2, 0)
    b_start = jnp.where(ha_even, 0, rows - 2)
    for which, ref in enumerate((x_ref, g_ref)):
        copies[which].wait()
        to_a[which] = ref[pl.ds(a_start, 2)]
        to_b[which] = ref[pl.ds(b_start, 2)]
        for r in range(rows):
            left, right = ref[r, 0:2, :], ref[r, cols - 2 : cols, :]
            own_a[which, r] = jnp.where(wa_even, right, left)
            own_b[which, r] = jnp.where(wa_even, left, right)
    for copy in copies[2:]:
        copy.wait()


def pack(x, g, one, two):
    rows, cols, lanes = x.shape
    vmem = pl.BlockSpec(memory_space=pltpu.VMEM)
    hbm = pl.BlockSpec(memory_space=pltpu.HBM)
    shapes = [x.shape] * 2 + [one.shape] * 2
    shapes += [(2, 2, cols, lanes)] * 2 + [(2, rows, 2, lanes)] * 2
    return pl.pallas_call(
        pack_kernel,
        out_shape=tuple(jax.ShapeDtypeStruct(shape, x.dtype) for shape in shapes),
        in_specs=[hbm] * 4,
        out_specs=(vmem,) * 8,
        scratch_shapes=[pltpu.SemaphoreType.DMA((4,))],
        compiler_params=pltpu.CompilerParams(vmem_limit_bytes=4 << 20),
        cost_estimate=pl.CostEstimate(flops=0, bytes_accessed=1_100_000, transcendentals=0),
    )(*(in_hbm(block) for block in (x, g, one, two)))


def corners_kernel(wa_ref, wb_ref, to_a, to_b):
    rows = wa_ref.shape[1]
    ha_even = lax.rem(lax.axis_index("ha"), 2) == 0
    a_start = jnp.where(ha_even, rows - 2, 0)
    b_start = jnp.where(ha_even, 0, rows - 2)
    for side, ref in enumerate((wa_ref, wb_ref)):
        for which in range(2):
            for r in range(2):
                to_a[side, which, r] = ref[which, a_start + r]
                to_b[side, which, r] = ref[which, b_start + r]


def small_call(kernel, out_shape, *operands):
    vmem = pl.BlockSpec(memory_space=pltpu.VMEM)
    return pl.pallas_call(
        kernel,
        out_shape=out_shape,
        in_specs=[vmem] * len(operands),
        out_specs=(vmem,) * len(out_shape),
        compiler_params=pltpu.CompilerParams(vmem_limit_bytes=2 << 20),
        cost_estimate=pl.CostEstimate(flops=0, bytes_accessed=300_000, transcendentals=0),
    )(*operands)


def corners(wa, wb):
    shape = jax.ShapeDtypeStruct((2, 2, 2) + wa.shape[2:], wa.dtype)
    return small_call(corners_kernel, (shape, shape), wa, wb)


def halo_selection(lines, shape):
    ha_odd = lax.rem(lax.axis_index("ha"), 2)
    wa_odd = lax.rem(lax.axis_index("wa"), 2)
    halo = 2 * lines
    gap_rows = (lines + 1) * PAD
    side_rows = 2 * lines
    q = lax.broadcasted_iota(jnp.int32, shape, 0)
    col = lax.broadcasted_iota(jnp.int32, shape, 1)

    def order(line):
        swapped = jnp.where(
            line < 2, line + lines - 2, jnp.where(line >= lines - 2, line - lines + 2, line)
        )
        return jnp.where(ha_odd == 0, swapped, line)

    left_base = jnp.where(wa_odd == 0, halo, 0)
    right_base = jnp.where(wa_odd == 0, 0, halo)
    gap = lax.div(q, PAD)
    w = lax.rem(q, PAD)
    left_hit = (w == PAD - 1) & (gap < lines) & (col == left_base + 2 * order(gap) + 1)
    right_hit = (w == 0) & (gap >= 1) & (col == right_base + 2 * order(gap - 1))
    in_gaps = (q < gap_rows) & (left_hit | right_hit)
    q = q - gap_rows
    tap = lax.div(q, side_rows)
    b = lax.rem(tap, 3)
    right = lax.div(lax.rem(q, side_rows), lines)
    line = lax.rem(q, lines) + lax.div(tap, 3) - 1
    at = order(line)
    left_source = jnp.where(b == 2, 2 * halo + at, left_base + 2 * at + b)
    right_source = jnp.where(b == 0, 2 * halo + lines + at, right_base + 2 * at + b - 1)
    source = jnp.where(right == 0, left_source, right_source)
    in_sides = (q >= 0) & (line >= 0) & (line < lines) & (col == source)
    return jnp.where(in_gaps | in_sides, 1.0, 0.0).astype(jnp.bfloat16)


def transposed(value, turned):
    flat = jnp.transpose(value)
    halves = []
    for side in range(flat.shape[1] // 128):
        turned[side] = flat[:, 128 * side : 128 * side + 128]
        pieces = [
            turned[side, pl.ds(64 * j + odd, 32, stride=2), :] for j in range(4) for odd in range(2)
        ]
        halves.append(jnp.concatenate(pieces, axis=0))
    return jnp.concatenate(halves, axis=1).astype(jnp.bfloat16)


def turn_lanes(parts):
    swapped = [pltpu.roll(part, CH, 1) for part in parts]
    low = lax.broadcasted_iota(jnp.int32, parts[0].shape, 1) < CH
    return [jnp.where(low, swapped[k - 1], swapped[k]) for k in range(len(parts))]


def gather_line(wide, wide_turned, slot, own, left, right, out, row):
    cols, lanes = own.shape
    tiles = lanes // 128
    nothing = lax.shift_right_logical(lax.axis_index("wa"), 16)
    base = slot * (cols + 2 * PAD)
    pieces = ((PAD - 1, 1, left), (PAD, cols, own), (PAD + cols, 1, right))
    for at, count, value in pieces:
        for k in range(tiles):
            wide[k, base + at : base + at + count, :] = value[:, 128 * k : 128 * k + 128]
    around = slice(base + PAD - 8, base + PAD + cols + 8)
    for k, value in enumerate(turn_lanes([wide[k, around, :] for k in range(tiles)])):
        wide_turned[k, around, :] = value
    start = base + PAD - 1
    plain, other = (
        [
            [ref[k, pl.ds(at, cols), :] for k in range(tiles)]
            for at in (start + nothing, start + 1, start + 2 + nothing)
        ]
        for ref in (wide, wide_turned)
    )
    for group, value in enumerate(gather_depths(plain, other)):
        out[group, row : row + cols, :] = value


def line_scratch(slots, cols, lanes):
    return [pltpu.VMEM((lanes // 128, slots * (cols + 2 * PAD), 128), jnp.float32)] * 2


def prepare_kernel(
    lines, x_ref, g_ref, wa_ref, wb_ref, one_ref, two_ref, one_out, two_flip_out, one_flip_out, select_out, xs_out, gs_out, wide, wide_turned
):
    select_out[...] = halo_selection(lines, select_out.shape)
    rows, cols, _ = x_ref.shape
    wa_even = lax.rem(lax.axis_index("wa"), 2) == 0
    for which, (ref, out) in enumerate(((x_ref, xs_out), (g_ref, gs_out))):
        for r in range(rows):
            near, far = (side[which, r].astype(jnp.float32) for side in (wa_ref, wb_ref))
            left, right = jnp.where(wa_even, far, near), jnp.where(wa_even, near, far)
            own = ref[r].astype(jnp.float32)
            slot = which * rows + r
            gather_line(wide, wide_turned, slot, own, left[1:2], right[:1], out, r * cols)
    zero = jnp.zeros((CH, CH), jnp.bfloat16)

    def banded(tiles):
        padded = [zero] + tiles + [zero]
        return [jnp.concatenate([padded[c + 1], padded[c]], axis=1) for c in range(4)]

    def flipped(ref, tap):
        return jnp.transpose(ref[26 - tap].astype(jnp.float32)).astype(jnp.bfloat16)

    for ab in range(9):
        taps = [3 * ab + c for c in range(3)]
        for c, tile in enumerate(banded([one_ref[t] for t in taps])):
            one_out[ab, c] = tile
        for c, tile in enumerate(banded([flipped(two_ref, t) for t in taps])):
            two_flip_out[ab, c] = tile
        for c, tile in enumerate(banded([flipped(one_ref, t) for t in taps])):
            one_flip_out[ab, c] = tile


def prepare(x, g, wa, wb, kernel_one, kernel_two):
    rows, cols, lanes = x.shape
    lines = rows + 4
    bands = jax.ShapeDtypeStruct((9, 4, CH, 2 * CH), jnp.bfloat16)
    select = ((lines + 1) * PAD + 18 * lines, 6 * lines)
    windows = jax.ShapeDtypeStruct((2, rows * cols, 1024), jnp.bfloat16)
    vmem = pl.BlockSpec(memory_space=pltpu.VMEM)
    return pl.pallas_call(
        functools.partial(prepare_kernel, lines),
        out_shape=(*[bands] * 3, jax.ShapeDtypeStruct(select, jnp.bfloat16), windows, windows),
        in_specs=[vmem] * 6,
        out_specs=(vmem,) * 6,
        scratch_shapes=line_scratch(2 * rows, cols, lanes),
        compiler_params=pltpu.CompilerParams(vmem_limit_bytes=12 << 20),
        cost_estimate=pl.CostEstimate(
            flops=4_000_000, bytes_accessed=4_000_000, transcendentals=0
        ),
    )(x, g, wa, wb, kernel_one, kernel_two)


def banded_weights(band_ref, group):
    zero = jnp.zeros((CH, 2 * CH), jnp.bfloat16)
    rows = []
    for ab in range(9):
        for i in range(5):
            halves = []
            for m in range(2):
                c = i - 2 * m + 1 - group
                halves.append(band_ref[ab, c] if 0 <= c < 4 else zero)
            rows.append(jnp.concatenate(halves, axis=1))
        if ab % 3 == 2:
            rows.append(jnp.concatenate([zero, zero], axis=1))
    return jnp.concatenate(rows, axis=0)


def gather_depths(plain, turned_lanes):
    zero = jnp.zeros_like(plain[0][0])
    low = lax.broadcasted_iota(jnp.int32, zero.shape, 1) < CH

    def part(tiles, k):
        return tiles[k]

    (p0, p1, p2), (t0, t1, t2) = plain, turned_lanes
    first = [
        part(p0, 0),
        part(p0, 1),
        jnp.where(low, part(p0, 2), part(t1, 0)),
        part(t1, 1),
        part(t1, 2),
        part(p2, 0),
        part(p2, 1),
        jnp.where(low, part(p2, 2), zero),
    ]
    second = [
        part(t0, 2),
        part(t0, 3),
        jnp.where(low, part(t0, 0), part(p1, 1)),
        part(p1, 2),
        part(p1, 3),
        part(t2, 2),
        part(t2, 3),
        jnp.where(low, part(t2, 0), zero),
    ]
    return [jnp.concatenate(half, axis=1).astype(jnp.bfloat16) for half in (first, second)]


def correlate(src, side, band_ref, cols, runs):
    outs = []
    for group in range(2):
        windows = []
        for a in range(3):
            parts = [
                src[group, (line + a - 1) * cols : (line + a - 1 + count) * cols, :]
                for line, count in runs
            ]
            if side is not None:
                parts.append(side[group, a])
            windows.append(parts[0] if len(parts) == 1 else jnp.concatenate(parts, axis=0))
        outs.append(
            jnp.dot(
                jnp.concatenate(windows, axis=1),
                banded_weights(band_ref, group),
                preferred_element_type=jnp.float32,
            )
        )
    return outs


def input_grad_kernel(rows, cols, ps, band_ref, out_ref):
    result = correlate(ps, None, band_ref, cols, [(2, rows)])
    for group in range(2):
        for r in range(rows):
            out_ref[r, :, 256 * group : 256 * group + 256] = result[group][
                r * cols : r * cols + cols
            ].astype(out_ref.dtype)


def field_tools(
    rows, cols, ra_ref, rb_ref, wa_ref, wb_ref, corner_a_ref, corner_b_ref, select_ref, scratch
):
    wide_refs, wide_turned_refs, edges_ref = scratch
    f32, bf16 = jnp.float32, jnp.bfloat16
    stride = cols + PAD
    lines = rows + 4
    base = 8
    ha = lax.axis_index("ha")
    wa = lax.axis_index("wa")
    ha_odd = lax.rem(ha, 2)
    wa_odd = lax.rem(wa, 2)

    nothing = lax.shift_right_logical(wa, 16)

    halo = 2 * lines
    gap_rows = (lines + 1) * PAD
    side_rows = 2 * lines

    tiles = ra_ref.shape[3] // 128

    def split_lanes(value):
        return [value[:, 128 * k : 128 * k + 128] for k in range(tiles)]

    def turn(parts):
        swapped = [pltpu.roll(part, CH, 1) for part in parts]
        low = lax.broadcasted_iota(jnp.int32, parts[0].shape, 1) < CH
        return [jnp.where(low, swapped[k - 1], swapped[k]) for k in range(tiles)]

    def put_wide(wide, start, count, parts, first=0):
        for k, part in enumerate(parts, first):
            wide[k, pl.ds(start, count), :] = part

    def gather_lines(which, first, last, out):
        wide, wide_turned = wide_refs[which], wide_turned_refs[which]
        top, bottom = base + first * stride, base + last * stride + PAD
        for k, value in enumerate(turn([wide[k, top - 8 : bottom + 8, :] for k in range(tiles)])):
            wide_turned[k, top - 8 : bottom + 8, :] = value
        for l in range(first, last):
            start = base + PAD + l * stride - 1
            where = [start + nothing, start + 1, start + 2 + nothing]
            plain, other = (
                [[ref[k, pl.ds(at, cols), :] for k in range(tiles)] for at in where]
                for ref in (wide, wide_turned)
            )
            for group, value in enumerate(gather_depths(plain, other)):
                out[group, l * cols : (l + 1) * cols, :] = value

    def spread(which, own_ref, out, side_out, gathered):
        wide, edges = wide_refs[which], edges_ref.at[which]
        for side, ref in enumerate((wa_ref, wb_ref)):
            pieces = (
                [corner_a_ref[side, which, r] for r in range(2)]
                + [ref[which, r] for r in range(rows)]
                + [corner_b_ref[side, which, r] for r in range(2)]
            )
            for k, piece in enumerate(pieces):
                top = side * halo + 2 * k
                edges[top : top + 2, :] = piece.astype(f32)
        owned = (
            [ra_ref[which, r].astype(f32) for r in range(2)]
            + [own_ref[r].astype(f32) for r in range(rows)]
            + [rb_ref[which, r].astype(f32) for r in range(2)]
        )
        for k, value in enumerate(owned):
            edges[2 * halo + k : 2 * halo + k + 1, :] = value[0:1, :]
            edges[2 * halo + lines + k : 2 * halo + lines + k + 1, :] = value[cols - 1 : cols, :]
        used = gap_rows if side_out is None else select_ref.shape[0]
        placed = jnp.dot(select_ref[:used], edges[...].astype(bf16), preferred_element_type=f32)
        for k in range(lines + 1):
            put_wide(wide, base + k * stride, PAD, split_lanes(placed[k * PAD : (k + 1) * PAD]))
        for r in range(rows):
            start = base + PAD + (r + 2) * stride
            put_wide(wide, start, cols, split_lanes(owned[r + 2]))
        above = base + PAD
        below = base + PAD + (rows + 2) * stride
        a_start = jnp.where(ha_odd == 0, below, above)
        b_start = jnp.where(ha_odd == 0, above, below)
        for r in range(2):
            put_wide(wide, pl.multiple_of(a_start + r * stride, 8), cols, split_lanes(owned[r]))
            put_wide(wide, pl.multiple_of(b_start + r * stride, 8), cols, split_lanes(owned[rows + 2 + r]))
        for first, last in gathered:
            gather_lines(which, first, last, out)
        for a in range(0 if side_out is None else 3):
            top = gap_rows + 3 * a * side_rows
            plain = [
                split_lanes(placed[top + b * side_rows : top + (b + 1) * side_rows])
                for b in range(3)
            ]
            other = [turn(parts) for parts in plain]
            for group, value in enumerate(gather_depths(plain, other)):
                side_out[group, a] = value

    return spread, gather_lines, put_wide, split_lanes


def own_windows(own, ends, group, cols, shift):
    if shift == 0:
        return own[group]
    count = own.shape[1]
    if shift < 0:
        return jnp.concatenate([ends[group, :cols, :], own[group, : count - cols, :]], axis=0)
    return jnp.concatenate([own[group, cols:, :], ends[group, cols:, :]], axis=0)


def correlate_own(own, ends, band_ref, cols, group):
    windows = [own_windows(own, ends, group, cols, a - 1) for a in range(3)]
    return jnp.dot(
        jnp.concatenate(windows, axis=1),
        banded_weights(band_ref, group),
        preferred_element_type=jnp.float32,
    )


def main_kernel(
    cols,
    ra_ref,
    rb_ref,
    corner_a_ref,
    corner_b_ref,
    xs,
    gs,
    one_ref,
    two_flip_ref,
    grad_pre_ref,
    *rest,
):
    f32, bf16 = jnp.float32, jnp.bfloat16
    kg_refs, scratch = rest[:-10], rest[-10:]
    x_ends, g_ends, sums, acc_one, acc_two, turned_refs = *scratch[:5], scratch[5:7]
    swap, wide, wide_turned = scratch[7:]
    ha_odd = lax.rem(lax.axis_index("ha"), 2)
    wa_odd = lax.rem(lax.axis_index("wa"), 2)
    nothing = lax.shift_right_logical(lax.axis_index("wa"), 16)

    def spread(which, out):
        for slot, (odd_refs, even_refs, r) in enumerate(
            (
                ((ra_ref, corner_a_ref), (rb_ref, corner_b_ref), 1),
                ((rb_ref, corner_b_ref), (ra_ref, corner_a_ref), 0),
            )
        ):
            own, left, right = (
                jnp.where(ha_odd == 1, odd.astype(f32), even.astype(f32))
                for odd, even in (
                    (odd_refs[0][which, r], even_refs[0][which, r]),
                    *(
                        (odd_refs[1][side, which, r], even_refs[1][side, which, r])
                        for side in (1 - wa_odd, wa_odd)
                    ),
                )
            )
            at = 2 * which + slot
            gather_line(wide, wide_turned, at, own, left[1:2], right[:1], out, slot * cols)

    spread(0, x_ends)
    spread(1, g_ends)
    pre = [correlate_own(xs, x_ends, one_ref, cols, group) for group in range(2)]
    grad_active = [correlate_own(gs, g_ends, two_flip_ref, cols, group) for group in range(2)]

    active_t, slopes = [], []
    for group in range(2):
        value = pre[group]
        cdf = 0.5 * (1.0 + lax.erf(value * root_half))
        slopes.append(cdf + value * inv_root_two_pi * jnp.exp(-0.5 * value * value))
        active_t.append(transposed(value * cdf, turned_refs[group]))

    half, lead = CH // 2, 8
    low_half = lax.broadcasted_iota(jnp.int32, (CH, 2 * CH), 1) < CH
    low = low_half[:half]

    def kernel_grad_parts(fixed, acc_ref, a):
        parts = [[None] * 4 for _ in range(3)]

        def put(window, e, tile):
            old = parts[2 - window][e]
            parts[2 - window][e] = tile if old is None else old + tile

        for group in range(2):
            window = own_windows(gs, g_ends, group, cols, 1 - a)
            acc = acc_ref.at[group]
            acc[...] = jnp.dot(fixed[group], window, preferred_element_type=f32)
            for j in range(4):
                for t in range(8):
                    (window, i), (next_window, next_i) = divmod(2 * t, 5), divmod(2 * t + 1, 5)
                    e = j - i + 1 + group
                    c = j - next_i + 1 + group
                    joined = next_window in (window, 3)
                    use_left = 0 <= e < 4 if joined else 0 <= e < 3
                    use_right = not joined and 0 <= c < 3
                    if not (use_left or use_right):
                        continue
                    tile = acc[64 * j : 64 * j + 64, 128 * t : 128 * t + 128]
                    if use_left:
                        whole = joined or e == 0
                        put(window, e, tile if whole else jnp.where(low_half, tile, 0.0))
                    if use_right:
                        whole = c == 2
                        put(next_window, c + 1, tile if whole else jnp.where(low_half, 0.0, tile))
        return parts

    def put_tile(k, tap, left, right):
        sums[k, lead + half * tap : lead + half * tap + half, :] = jnp.where(low, left, right)

    def add_taps(a, parts):
        for b in range(3):
            for c in range(3):
                left, right = parts[b][c], parts[b][c + 1]
                put_tile(
                    1,
                    9 * a + 3 * b + c,
                    left[:half] + pltpu.roll(right[:half], CH, 1),
                    pltpu.roll(left[half:], CH, 1) + right[half:],
                )

    def first_grad(fixed, a):
        parts = [[None] * 4 for _ in range(3)]

        def put(window, e, tile):
            old = parts[window][e + 1]
            parts[window][e + 1] = tile if old is None else old + tile

        for group in range(2):
            window = own_windows(xs, x_ends, group, cols, a - 1)
            acc_ref = acc_one.at[2 * a + group]
            acc_ref[...] = jnp.dot(fixed[group], window, preferred_element_type=f32)
            for j in range(4):
                for t in range(8):
                    (window, i), (next_window, next_i) = divmod(2 * t, 5), divmod(2 * t + 1, 5)
                    e = i - j + 1 - group
                    c = next_i - j + 1 - group
                    joined = next_window in (window, 3)
                    use_left = -1 <= e < 3 if joined else 0 <= e < 3
                    use_right = not joined and 0 <= c < 3
                    if not (use_left or use_right):
                        continue
                    tile = acc_ref[64 * j : 64 * j + 64, 128 * t : 128 * t + 128]
                    if use_left:
                        whole = joined or e == 2
                        put(window, e, tile if whole else jnp.where(low_half, tile, 0.0))
                    if use_right:
                        whole = c == 0
                        put(next_window, c - 1, tile if whole else jnp.where(low_half, 0.0, tile))

        def joined_halves(b, c, d):
            first = parts[b][c + 1] + pltpu.roll(parts[b][c], CH, 1)
            second = pltpu.roll(parts[b][d + 1], CH, 1) + parts[b][d]
            return jnp.where(low_half, first, second)

        for b in range(3):
            for k, (c, d) in enumerate(((0, 1), (2, 2))):
                slot = swap.at[2 * (3 * a + b) + k]
                slot[:, :CH] = jnp.transpose(joined_halves(b, c, d))
                for tap, at in ((c, 0), (d, CH))[: 1 + (c != d)]:
                    even = slot[pl.ds(at, half, stride=2), :]
                    odd = slot[pl.ds(at + 1, half, stride=2), :]
                    put_tile(0, 9 * a + 3 * b + tap, even, pltpu.roll(odd, CH, 1))

    add_taps(0, kernel_grad_parts(active_t, acc_two.at[0], 0))
    grad_pre_t = []
    for group in range(2):
        grad_pre = grad_active[group] * slopes[group]
        grad_pre_ref[:, 256 * group : 256 * group + 256] = grad_pre.astype(bf16)
        grad_pre_t.append(jnp.transpose(grad_pre).astype(bf16))
    for a in range(3):
        first_grad(grad_pre_t, a)
    for a in (1, 2):
        add_taps(a, kernel_grad_parts(active_t, acc_two.at[a], a))

    if len(kg_refs) == 1:
        for k in range(2):
            kg_refs[0][k] = sums[k, lead : lead + 27 * half, :]
        return
    keep_ref, send_ref = kg_refs
    slabs, width, share, _ = keep_ref.shape
    take = 27 * half // (2 * slabs * width)
    full, left_over = take // 8 * 8, take % 8
    head = lax.broadcasted_iota(jnp.int32, (8, 2 * CH), 0) < left_over

    def chunk(d):
        at = lead + take * d + nothing
        first = sums[0, pl.ds(at, full + 8), :]
        second = sums[1, pl.ds(at - left_over, share - full), :]
        seam = jnp.where(head, first[full:], second[:8])
        return jnp.concatenate([first[:full], seam, second[8:]], axis=0)

    for z in range(slabs):
        for w in range(width):
            even, odd = (chunk((2 * z + c) * width + w) for c in range(2))
            keep_ref[z, w] = jnp.where(ha_odd == 0, even, odd)
            send_ref[z, w] = jnp.where(ha_odd == 0, odd, even).astype(bf16)


def ring_kernel(
    rows,
    cols,
    x_ref,
    g_ref,
    ra_ref,
    rb_ref,
    wa_ref,
    wb_ref,
    corner_a_ref,
    corner_b_ref,
    select_ref,
    one_ref,
    two_flip_ref,
    grad_pre_ref,
    ps,
    *scratch,
):
    f32 = jnp.float32
    xs, gs, x_side, g_side = scratch[:4]
    wide_refs, edges_ref = scratch[4:7], scratch[10]
    spread, gather_lines, put_wide, split_lanes = field_tools(
        rows,
        cols,
        ra_ref,
        rb_ref,
        wa_ref,
        wb_ref,
        corner_a_ref,
        corner_b_ref,
        select_ref,
        (wide_refs, scratch[7:10], edges_ref),
    )
    lines, stride, base = rows + 4, cols + PAD, 8
    side_rows = 2 * lines
    ha, wa = lax.axis_index("ha"), lax.axis_index("wa")
    ha_last = lax.axis_size("ha") - 1
    wa_last = lax.axis_size("wa") - 1
    runs = [(1, 1), (rows + 2, 1)]
    gathered = [(0, 3), (lines - 3, lines)]
    spread(0, x_ref, xs, x_side, gathered)
    pre = correlate(xs, x_side, one_ref, cols, runs)
    spread(1, g_ref, gs, g_side, gathered)
    grad_active = correlate(gs, g_side, two_flip_ref, cols, runs)
    position = lax.broadcasted_iota(jnp.int32, (side_rows, 256), 0)
    line = lax.rem(position, lines)
    dead = ((line < 2) & (ha == 0)) | ((line >= rows + 2) & (ha == ha_last))
    dead = dead | ((position < lines) & (wa == 0)) | ((position >= lines) & (wa == wa_last))
    wide, edges = wide_refs[2], edges_ref.at[2]
    for r in range(rows):
        own = grad_pre_ref[r * cols : r * cols + cols, :].astype(f32)
        put_wide(wide, base + PAD + (r + 2) * stride, cols, split_lanes(own))
    for group in range(2):
        value = pre[group]
        cdf = 0.5 * (1.0 + lax.erf(value * root_half))
        slope = cdf + value * inv_root_two_pi * jnp.exp(-0.5 * value * value)
        grad_pre = grad_active[group] * slope
        above = jnp.where(ha == 0, 0.0, grad_pre[:cols])
        below = jnp.where(ha == ha_last, 0.0, grad_pre[cols : 2 * cols])
        for l, part in ((1, above), (rows + 2, below)):
            start = base + PAD + l * stride
            put_wide(wide, start, cols, [part[:, :128], part[:, 128:]], 2 * group)
        edges[:side_rows, 256 * group : 256 * group + 256] = jnp.where(
            dead, 0.0, grad_pre[2 * cols :]
        )
    for l in range(1, rows + 3):
        left, right = base + l * stride + PAD - 1, base + (l + 1) * stride
        put_wide(wide, left, 1, split_lanes(edges[l : l + 1, :]))
        put_wide(wide, right, 1, split_lanes(edges[lines + l : lines + l + 1, :]))
    gather_lines(2, 1, rows + 3, ps)


def scratch_shapes(rows, cols, lanes, fields):
    span = (rows + 4) * (cols + PAD) + PAD
    wide = pltpu.VMEM((lanes // 128, span + 16, 128), jnp.float32)
    return [*[wide] * (2 * fields), pltpu.VMEM((fields, 6 * (rows + 4), lanes), jnp.float32)]


def main(shape, operands, split):
    rows, cols, lanes = shape
    if split:
        slabs, width = split
        take = 27 * CH // 2 // (2 * slabs * width)
        share = -(-2 * take // 8) * 8
        grads = tuple(
            jax.ShapeDtypeStruct((slabs, width, share, 2 * CH), dtype)
            for dtype in (jnp.float32, jnp.bfloat16)
        )
    else:
        grads = (jax.ShapeDtypeStruct((2, 27 * CH // 2, 2 * CH), jnp.float32),)
    vmem = pl.BlockSpec(memory_space=pltpu.VMEM)
    ends = pltpu.VMEM((2, 2 * cols, 1024), jnp.bfloat16)
    turning = pltpu.VMEM((rows * cols // 128, 256, 128), jnp.float32)
    return pl.pallas_call(
        functools.partial(main_kernel, cols),
        out_shape=(jax.ShapeDtypeStruct((rows * cols, lanes), jnp.bfloat16), *grads),
        in_specs=[vmem] * 8,
        out_specs=(vmem,) * (1 + len(grads)),
        scratch_shapes=[
            ends,
            ends,
            pltpu.VMEM((2, 27 * CH // 2 + 40, 2 * CH), jnp.float32),
            pltpu.VMEM((6, 256, 1024), jnp.float32),
            pltpu.VMEM((3, 2, 256, 1024), jnp.float32),
            turning,
            turning,
            pltpu.VMEM((18, 2 * CH, 2 * CH), jnp.float32),
            *line_scratch(4, cols, lanes),
        ],
        compiler_params=pltpu.CompilerParams(vmem_limit_bytes=32 << 20),
        cost_estimate=pl.CostEstimate(
            flops=10_000_000_000, bytes_accessed=8_000_000, transcendentals=1_000_000
        ),
    )(*operands)


def ring(fields, bands, grad_pre):
    rows, cols, lanes = fields[0].shape
    vmem = pl.BlockSpec(memory_space=pltpu.VMEM)
    moving = ((2, (rows + 4) * cols, 1024), jnp.bfloat16)
    side = pltpu.VMEM((2, 3, 2 * (rows + 4), 1024), jnp.bfloat16)
    return pl.pallas_call(
        functools.partial(ring_kernel, rows, cols),
        out_shape=jax.ShapeDtypeStruct(*moving),
        in_specs=[vmem] * 12,
        out_specs=vmem,
        scratch_shapes=[
            pltpu.VMEM(*moving),
            pltpu.VMEM(*moving),
            side,
            side,
            *scratch_shapes(rows, cols, lanes, 3),
        ],
        compiler_params=pltpu.CompilerParams(vmem_limit_bytes=20 << 20),
        cost_estimate=pl.CostEstimate(
            flops=3_000_000_000, bytes_accessed=8_000_000, transcendentals=500_000
        ),
    )(*fields, *bands, grad_pre)


def input_grad(ps, band, shape):
    rows, cols, _ = shape
    vmem = pl.BlockSpec(memory_space=pltpu.VMEM)
    return pl.pallas_call(
        functools.partial(input_grad_kernel, rows, cols),
        out_shape=jax.ShapeDtypeStruct(shape, jnp.bfloat16),
        in_specs=[vmem, vmem],
        out_specs=vmem,
        compiler_params=pltpu.CompilerParams(vmem_limit_bytes=8 << 20),
        cost_estimate=pl.CostEstimate(
            flops=2_000_000_000, bytes_accessed=4_000_000, transcendentals=0
        ),
    )(ps, band)


def xor_exchange(block, axis, mask):
    count = lax.axis_size(axis)
    return lax.ppermute(block, axis, [(i, i ^ mask) for i in range(count)])


def total_of(refs):
    total = refs[0].astype(jnp.float32)
    for ref in refs[1:]:
        total = total + ref.astype(jnp.float32)
    return total


def sum_chip_kernel(keep_ref, got_ref, own_ref, *send_refs):
    wa = lax.axis_index("wa")
    for z in range(keep_ref.shape[0]):
        own_ref[z] = total_of([keep_ref[z, wa], got_ref[z, wa]])
        for k, ref in enumerate(send_refs, 1):
            ref[z] = total_of([keep_ref[z, wa ^ k], got_ref[z, wa ^ k]]).astype(ref.dtype)


def sum_wa_kernel(*refs):
    slabs = refs[0].shape[0]
    got_refs, (own_ref, *send_refs) = refs[:-slabs], refs[-slabs:]
    z = lax.div(lax.axis_index("ha"), 2)
    own_ref[...] = total_of([ref[z] for ref in got_refs])
    for k, ref in enumerate(send_refs, 1):
        ref[...] = total_of([got[z ^ k] for got in got_refs]).astype(ref.dtype)


def sum_z_kernel(*refs):
    total = total_of([ref[...] for ref in refs[:-2]])
    take = refs[-1].shape[0]
    for k, ref in enumerate(refs[-2:]):
        ref[...] = total[k * take : (k + 1) * take]


def reduce_chunks(keep, send, take):
    slabs, width = keep.shape[:2]
    f32, bf16 = jnp.float32, jnp.bfloat16
    unit = keep.shape[2:]
    got = xor_exchange(send, "ha", 1)
    shapes = [jax.ShapeDtypeStruct((slabs,) + unit, f32)]
    shapes += [jax.ShapeDtypeStruct((slabs,) + unit, bf16)] * (width - 1)
    own, *sends = small_call(sum_chip_kernel, tuple(shapes), keep, got)
    got = []
    for k, block in enumerate(sends, 1):
        got.append(xor_exchange(block, "wa", k))
    shapes = [jax.ShapeDtypeStruct(unit, f32)]
    shapes += [jax.ShapeDtypeStruct(unit, f32)] * (slabs - 1)
    own, *sends = small_call(sum_wa_kernel, tuple(shapes), own, *got)
    got = []
    for k, block in enumerate(sends, 1):
        got.append(xor_exchange(block, "ha", 2 * k))
    shapes = (jax.ShapeDtypeStruct((take, 2 * CH), f32),) * 2
    return small_call(sum_z_kernel, shapes, own, *got)


def shards(inputs, grad_out, kernel_one, kernel_two):
    height_count = lax.axis_size("ha")
    width_count = lax.axis_size("wa")
    devices = height_count * width_count
    x, g, kernel_one, kernel_two, to_a, to_b, own_a, own_b = pack(
        inputs, grad_out, kernel_one, kernel_two
    )
    wb = pair_exchange(own_b, "wa", 1)
    wa = pair_exchange(own_a, "wa", 0)
    ra = pair_exchange(to_a, "ha", 0)
    rb = pair_exchange(to_b, "ha", 1)
    one, two_flip, one_flip, select, xs, gs = prepare(x, g, wa, wb, kernel_one, kernel_two)
    corner_to_a, corner_to_b = corners(wa, wb)
    corner_b = pair_exchange(corner_to_b, "ha", 1)
    corner_a = pair_exchange(corner_to_a, "ha", 0)

    split = None
    if (
        (27 * CH // 2) % devices == 0
        and height_count & (height_count - 1) == 0
        and width_count & (width_count - 1) == 0
        and height_count > 1
    ):
        split = (height_count // 2, width_count)
    fields = (x, g, ra, rb, wa, wb, corner_a, corner_b)
    bands = (select, one, two_flip)
    operands = (ra, rb, corner_a, corner_b, xs, gs, one, two_flip)
    grad_pre, *grads = main(inputs.shape, operands, split)
    ps = ring(fields, bands, grad_pre)
    grad_inputs = input_grad(ps, one_flip, inputs.shape)
    if split:
        grads = reduce_chunks(*grads, 27 * CH // 2 // devices)
    else:
        grads = [
            lax.psum_scatter(
                grads[0][k].reshape(devices, -1), ("ha", "wa"), scatter_dimension=0, tiled=True
            )
            for k in range(2)
        ]
    return (grad_inputs, grads[0].reshape(-1), grads[1].reshape(-1))


def solution(mesh):
    return jax.shard_map(
        shards,
        mesh=mesh,
        in_specs=(P("ha", "wa", None), P("ha", "wa", None), P(), P()),
        out_specs=(P("ha", "wa", None), P(("ha", "wa")), P(("ha", "wa"))),
        check_vma=False,
    )
```

```python
import functools

import jax
import jax.numpy as jnp
from jax import lax
from jax.experimental import pallas as pl
from jax.experimental.pallas import tpu as pltpu
from jax.sharding import PartitionSpec as P


CH = 64
PAD = 16

root_half = 0.7071067811865476
inv_root_two_pi = 0.3989422804014327


def pair_exchange(block, axis, first):
    count = lax.axis_size(axis)
    pairs = []
    for low in range(first, count - 1, 2):
        pairs += [(low, low + 1), (low + 1, low)]
    return lax.ppermute(block, axis, pairs)


def in_hbm(block):
    return pltpu.with_memory_space_constraint(block, pltpu.HBM)


def pack_kernel(
    x_hbm, g_hbm, x_ref, g_ref, to_a, to_b, own_a, own_b, sems
):
    rows, cols, _ = x_ref.shape
    pairs = ((x_hbm, x_ref), (g_hbm, g_ref))
    copies = [
        pltpu.make_async_copy(source, target, sems.at[k])
        for k, (source, target) in enumerate(pairs)
    ]
    for copy in copies:
        copy.start()
    ha_even = lax.rem(lax.axis_index("ha"), 2) == 0
    wa_even = lax.rem(lax.axis_index("wa"), 2) == 0
    a_start = jnp.where(ha_even, rows - 2, 0)
    b_start = jnp.where(ha_even, 0, rows - 2)
    for which, ref in enumerate((x_ref, g_ref)):
        copies[which].wait()
        to_a[which] = ref[pl.ds(a_start, 2)]
        to_b[which] = ref[pl.ds(b_start, 2)]
        for r in range(rows):
            left, right = ref[r, 0:2, :], ref[r, cols - 2 : cols, :]
            own_a[which, r] = jnp.where(wa_even, right, left)
            own_b[which, r] = jnp.where(wa_even, left, right)


def pack(x, g):
    rows, cols, lanes = x.shape
    vmem = pl.BlockSpec(memory_space=pltpu.VMEM)
    hbm = pl.BlockSpec(memory_space=pltpu.HBM)
    shapes = [x.shape] * 2
    shapes += [(2, 2, cols, lanes)] * 2 + [(2, rows, 2, lanes)] * 2
    return pl.pallas_call(
        pack_kernel,
        out_shape=tuple(jax.ShapeDtypeStruct(shape, x.dtype) for shape in shapes),
        in_specs=[hbm] * 2,
        out_specs=(vmem,) * 6,
        scratch_shapes=[pltpu.SemaphoreType.DMA((2,))],
        compiler_params=pltpu.CompilerParams(vmem_limit_bytes=4 << 20),
        cost_estimate=pl.CostEstimate(flops=0, bytes_accessed=1_100_000, transcendentals=0),
    )(*(in_hbm(block) for block in (x, g)))


def corners_kernel(wa_ref, wb_ref, to_a, to_b):
    rows = wa_ref.shape[1]
    ha_even = lax.rem(lax.axis_index("ha"), 2) == 0
    a_start = jnp.where(ha_even, rows - 2, 0)
    b_start = jnp.where(ha_even, 0, rows - 2)
    for side, ref in enumerate((wa_ref, wb_ref)):
        for which in range(2):
            for r in range(2):
                to_a[side, which, r] = ref[which, a_start + r]
                to_b[side, which, r] = ref[which, b_start + r]


def small_call(kernel, out_shape, *operands):
    vmem = pl.BlockSpec(memory_space=pltpu.VMEM)
    return pl.pallas_call(
        kernel,
        out_shape=out_shape,
        in_specs=[vmem] * len(operands),
        out_specs=(vmem,) * len(out_shape),
        compiler_params=pltpu.CompilerParams(vmem_limit_bytes=2 << 20),
        cost_estimate=pl.CostEstimate(flops=0, bytes_accessed=300_000, transcendentals=0),
    )(*operands)


def corners(wa, wb):
    shape = jax.ShapeDtypeStruct((2, 2, 2) + wa.shape[2:], wa.dtype)
    return small_call(corners_kernel, (shape, shape), wa, wb)


def halo_selection(lines, shape):
    ha_odd = lax.rem(lax.axis_index("ha"), 2)
    wa_odd = lax.rem(lax.axis_index("wa"), 2)
    halo = 2 * lines
    gap_rows = (lines + 1) * PAD
    side_rows = 2 * lines
    q = lax.broadcasted_iota(jnp.int32, shape, 0)
    col = lax.broadcasted_iota(jnp.int32, shape, 1)

    def order(line):
        swapped = jnp.where(
            line < 2, line + lines - 2, jnp.where(line >= lines - 2, line - lines + 2, line)
        )
        return jnp.where(ha_odd == 0, swapped, line)

    left_base = jnp.where(wa_odd == 0, halo, 0)
    right_base = jnp.where(wa_odd == 0, 0, halo)
    gap = lax.div(q, PAD)
    w = lax.rem(q, PAD)
    left_hit = (w == PAD - 1) & (gap < lines) & (col == left_base + 2 * order(gap) + 1)
    right_hit = (w == 0) & (gap >= 1) & (col == right_base + 2 * order(gap - 1))
    in_gaps = (q < gap_rows) & (left_hit | right_hit)
    q = q - gap_rows
    tap = lax.div(q, side_rows)
    b = lax.rem(tap, 3)
    right = lax.div(lax.rem(q, side_rows), lines)
    line = lax.rem(q, lines) + lax.div(tap, 3) - 1
    at = order(line)
    left_source = jnp.where(b == 2, 2 * halo + at, left_base + 2 * at + b)
    right_source = jnp.where(b == 0, 2 * halo + lines + at, right_base + 2 * at + b - 1)
    source = jnp.where(right == 0, left_source, right_source)
    in_sides = (q >= 0) & (line >= 0) & (line < lines) & (col == source)
    return jnp.where(in_gaps | in_sides, 1.0, 0.0).astype(jnp.bfloat16)


def transposed(value, turned):
    flat = jnp.transpose(value)
    halves = []
    for side in range(flat.shape[1] // 128):
        turned[side] = flat[:, 128 * side : 128 * side + 128]
        pieces = [
            turned[side, pl.ds(64 * j + odd, 32, stride=2), :] for j in range(4) for odd in range(2)
        ]
        halves.append(jnp.concatenate(pieces, axis=0))
    return jnp.concatenate(halves, axis=1).astype(jnp.bfloat16)


def turn_lanes(parts):
    swapped = [pltpu.roll(part, CH, 1) for part in parts]
    low = lax.broadcasted_iota(jnp.int32, parts[0].shape, 1) < CH
    return [jnp.where(low, swapped[k - 1], swapped[k]) for k in range(len(parts))]


def gather_line(wide, wide_turned, slot, own, left, right, out, row):
    cols, lanes = own.shape
    tiles = lanes // 128
    nothing = lax.shift_right_logical(lax.axis_index("wa"), 16)
    base = slot * (cols + 2 * PAD)
    pieces = ((PAD - 1, 1, left), (PAD, cols, own), (PAD + cols, 1, right))
    for at, count, value in pieces:
        for k in range(tiles):
            wide[k, base + at : base + at + count, :] = value[:, 128 * k : 128 * k + 128]
    around = slice(base + PAD - 8, base + PAD + cols + 8)
    for k, value in enumerate(turn_lanes([wide[k, around, :] for k in range(tiles)])):
        wide_turned[k, around, :] = value
    start = base + PAD - 1
    plain, other = (
        [
            [ref[k, pl.ds(at, cols), :] for k in range(tiles)]
            for at in (start + nothing, start + 1, start + 2 + nothing)
        ]
        for ref in (wide, wide_turned)
    )
    for group, value in enumerate(gather_depths(plain, other)):
        out[group, row : row + cols, :] = value


def line_scratch(slots, cols, lanes):
    return [pltpu.VMEM((lanes // 128, slots * (cols + 2 * PAD), 128), jnp.float32)] * 2


def put_band(out, ab, tiles):
    zero = jnp.zeros((CH, CH), jnp.bfloat16)
    padded = [zero, *tiles, zero]
    for c in range(4):
        out[ab, c] = jnp.concatenate([padded[c + 1], padded[c]], axis=1)


def flipped_taps(ref, ab):
    taps = [ref[26 - 3 * ab - c].astype(jnp.float32) for c in range(3)]
    return [jnp.transpose(tap).astype(jnp.bfloat16) for tap in taps]


def prepare_kernel(
    x_ref,
    g_ref,
    wa_ref,
    wb_ref,
    one_hbm,
    two_hbm,
    one_out,
    two_flip_out,
    xs_out,
    gs_out,
    one_ref,
    two_ref,
    wide,
    wide_turned,
    sems,
):
    copies = [
        pltpu.make_async_copy(one_hbm, one_ref, sems.at[0]),
        pltpu.make_async_copy(two_hbm, two_ref, sems.at[1]),
    ]
    for copy in copies:
        copy.start()
    rows, cols, _ = x_ref.shape
    wa_even = lax.rem(lax.axis_index("wa"), 2) == 0
    for which, (ref, out) in enumerate(((x_ref, xs_out), (g_ref, gs_out))):
        for r in range(rows):
            near, far = (side[which, r].astype(jnp.float32) for side in (wa_ref, wb_ref))
            left, right = jnp.where(wa_even, far, near), jnp.where(wa_even, near, far)
            own = ref[r].astype(jnp.float32)
            slot = which * rows + r
            gather_line(wide, wide_turned, slot, own, left[1:2], right[:1], out, r * cols)
    for copy in copies:
        copy.wait()
    for ab in range(9):
        put_band(one_out, ab, [one_ref[3 * ab + c] for c in range(3)])
        put_band(two_flip_out, ab, flipped_taps(two_ref, ab))


def prepare(x, g, wa, wb, kernel_one, kernel_two):
    rows, cols, lanes = x.shape
    bands = jax.ShapeDtypeStruct((9, 4, CH, 2 * CH), jnp.bfloat16)
    windows = jax.ShapeDtypeStruct((2, rows * cols, 1024), jnp.bfloat16)
    vmem = pl.BlockSpec(memory_space=pltpu.VMEM)
    return pl.pallas_call(
        prepare_kernel,
        out_shape=(bands, bands, windows, windows),
        in_specs=[vmem] * 4 + [pl.BlockSpec(memory_space=pltpu.HBM)] * 2,
        out_specs=(vmem,) * 4,
        scratch_shapes=[
            pltpu.VMEM(kernel_one.shape, kernel_one.dtype),
            pltpu.VMEM(kernel_two.shape, kernel_two.dtype),
            *line_scratch(2 * rows, cols, lanes),
            pltpu.SemaphoreType.DMA((2,)),
        ],
        compiler_params=pltpu.CompilerParams(vmem_limit_bytes=12 << 20),
        cost_estimate=pl.CostEstimate(
            flops=4_000_000, bytes_accessed=4_000_000, transcendentals=0
        ),
    )(x, g, wa, wb, in_hbm(kernel_one), in_hbm(kernel_two))


def banded_weights(band_ref, group):
    zero = jnp.zeros((CH, 2 * CH), jnp.bfloat16)
    rows = []
    for ab in range(9):
        for i in range(5):
            halves = []
            for m in range(2):
                c = i - 2 * m + 1 - group
                halves.append(band_ref[ab, c] if 0 <= c < 4 else zero)
            rows.append(jnp.concatenate(halves, axis=1))
        if ab % 3 == 2:
            rows.append(jnp.concatenate([zero, zero], axis=1))
    return jnp.concatenate(rows, axis=0)


def gather_depths(plain, turned_lanes):
    zero = jnp.zeros_like(plain[0][0])
    low = lax.broadcasted_iota(jnp.int32, zero.shape, 1) < CH

    def part(tiles, k):
        return tiles[k]

    (p0, p1, p2), (t0, t1, t2) = plain, turned_lanes
    first = [
        part(p0, 0),
        part(p0, 1),
        jnp.where(low, part(p0, 2), part(t1, 0)),
        part(t1, 1),
        part(t1, 2),
        part(p2, 0),
        part(p2, 1),
        jnp.where(low, part(p2, 2), zero),
    ]
    second = [
        part(t0, 2),
        part(t0, 3),
        jnp.where(low, part(t0, 0), part(p1, 1)),
        part(p1, 2),
        part(p1, 3),
        part(t2, 2),
        part(t2, 3),
        jnp.where(low, part(t2, 0), zero),
    ]
    return [jnp.concatenate(half, axis=1).astype(jnp.bfloat16) for half in (first, second)]


def correlate(src, side, band_ref, cols, runs):
    outs = []
    for group in range(2):
        windows = []
        for a in range(3):
            parts = [
                src[group, (line + a - 1) * cols : (line + a - 1 + count) * cols, :]
                for line, count in runs
            ]
            if side is not None:
                parts.append(side[group, a])
            windows.append(parts[0] if len(parts) == 1 else jnp.concatenate(parts, axis=0))
        outs.append(
            jnp.dot(
                jnp.concatenate(windows, axis=1),
                banded_weights(band_ref, group),
                preferred_element_type=jnp.float32,
            )
        )
    return outs


def input_grad_kernel(rows, cols, ps, one_ref, out_ref, band_ref):
    for ab in range(9):
        put_band(band_ref, ab, flipped_taps(one_ref, ab))
    result = correlate(ps, None, band_ref, cols, [(2, rows)])
    for group in range(2):
        for r in range(rows):
            out_ref[r, :, 256 * group : 256 * group + 256] = result[group][
                r * cols : r * cols + cols
            ].astype(out_ref.dtype)


def field_tools(
    rows, cols, ra_ref, rb_ref, wa_ref, wb_ref, corner_a_ref, corner_b_ref, select_ref, scratch
):
    wide_refs, wide_turned_refs, edges_ref = scratch
    f32, bf16 = jnp.float32, jnp.bfloat16
    stride = cols + PAD
    lines = rows + 4
    base = 8
    ha = lax.axis_index("ha")
    wa = lax.axis_index("wa")
    ha_odd = lax.rem(ha, 2)
    wa_odd = lax.rem(wa, 2)

    nothing = lax.shift_right_logical(wa, 16)

    halo = 2 * lines
    gap_rows = (lines + 1) * PAD
    side_rows = 2 * lines

    tiles = ra_ref.shape[3] // 128

    def split_lanes(value):
        return [value[:, 128 * k : 128 * k + 128] for k in range(tiles)]

    def turn(parts):
        swapped = [pltpu.roll(part, CH, 1) for part in parts]
        low = lax.broadcasted_iota(jnp.int32, parts[0].shape, 1) < CH
        return [jnp.where(low, swapped[k - 1], swapped[k]) for k in range(tiles)]

    def put_wide(wide, start, count, parts, first=0):
        for k, part in enumerate(parts, first):
            wide[k, pl.ds(start, count), :] = part

    def gather_lines(which, first, last, out):
        wide, wide_turned = wide_refs[which], wide_turned_refs[which]
        top, bottom = base + first * stride, base + last * stride + PAD
        for k, value in enumerate(turn([wide[k, top - 8 : bottom + 8, :] for k in range(tiles)])):
            wide_turned[k, top - 8 : bottom + 8, :] = value
        for l in range(first, last):
            start = base + PAD + l * stride - 1
            where = [start + nothing, start + 1, start + 2 + nothing]
            plain, other = (
                [[ref[k, pl.ds(at, cols), :] for k in range(tiles)] for at in where]
                for ref in (wide, wide_turned)
            )
            for group, value in enumerate(gather_depths(plain, other)):
                out[group, l * cols : (l + 1) * cols, :] = value

    def spread(which, own_ref, out, side_out, gathered):
        wide, edges = wide_refs[which], edges_ref.at[which]
        for side, ref in enumerate((wa_ref, wb_ref)):
            pieces = (
                [corner_a_ref[side, which, r] for r in range(2)]
                + [ref[which, r] for r in range(rows)]
                + [corner_b_ref[side, which, r] for r in range(2)]
            )
            for k, piece in enumerate(pieces):
                top = side * halo + 2 * k
                edges[top : top + 2, :] = piece.astype(f32)
        owned = (
            [ra_ref[which, r].astype(f32) for r in range(2)]
            + [own_ref[r].astype(f32) for r in range(rows)]
            + [rb_ref[which, r].astype(f32) for r in range(2)]
        )
        for k, value in enumerate(owned):
            edges[2 * halo + k : 2 * halo + k + 1, :] = value[0:1, :]
            edges[2 * halo + lines + k : 2 * halo + lines + k + 1, :] = value[cols - 1 : cols, :]
        used = gap_rows if side_out is None else select_ref.shape[0]
        placed = jnp.dot(select_ref[:used], edges[...].astype(bf16), preferred_element_type=f32)
        for k in range(lines + 1):
            put_wide(wide, base + k * stride, PAD, split_lanes(placed[k * PAD : (k + 1) * PAD]))
        for r in range(rows):
            start = base + PAD + (r + 2) * stride
            put_wide(wide, start, cols, split_lanes(owned[r + 2]))
        above = base + PAD
        below = base + PAD + (rows + 2) * stride
        a_start = jnp.where(ha_odd == 0, below, above)
        b_start = jnp.where(ha_odd == 0, above, below)
        for r in range(2):
            put_wide(wide, pl.multiple_of(a_start + r * stride, 8), cols, split_lanes(owned[r]))
            put_wide(wide, pl.multiple_of(b_start + r * stride, 8), cols, split_lanes(owned[rows + 2 + r]))
        for first, last in gathered:
            gather_lines(which, first, last, out)
        for a in range(0 if side_out is None else 3):
            top = gap_rows + 3 * a * side_rows
            plain = [
                split_lanes(placed[top + b * side_rows : top + (b + 1) * side_rows])
                for b in range(3)
            ]
            other = [turn(parts) for parts in plain]
            for group, value in enumerate(gather_depths(plain, other)):
                side_out[group, a] = value

    return spread, gather_lines, put_wide, split_lanes


def own_windows(own, ends, group, cols, shift):
    if shift == 0:
        return own[group]
    count = own.shape[1]
    if shift < 0:
        return jnp.concatenate([ends[group, :cols, :], own[group, : count - cols, :]], axis=0)
    return jnp.concatenate([own[group, cols:, :], ends[group, cols:, :]], axis=0)


def correlate_own(own, ends, band_ref, cols, group):
    windows = [own_windows(own, ends, group, cols, a - 1) for a in range(3)]
    return jnp.dot(
        jnp.concatenate(windows, axis=1),
        banded_weights(band_ref, group),
        preferred_element_type=jnp.float32,
    )


def main_kernel(
    cols,
    ra_ref,
    rb_ref,
    corner_a_ref,
    corner_b_ref,
    xs,
    gs,
    one_ref,
    two_flip_ref,
    grad_pre_ref,
    *rest,
):
    f32, bf16 = jnp.float32, jnp.bfloat16
    kg_refs, scratch = rest[:-10], rest[-10:]
    x_ends, g_ends, sums, acc_one, acc_two, turned_refs = *scratch[:5], scratch[5:7]
    swap, wide, wide_turned = scratch[7:]
    ha_odd = lax.rem(lax.axis_index("ha"), 2)
    wa_odd = lax.rem(lax.axis_index("wa"), 2)
    nothing = lax.shift_right_logical(lax.axis_index("wa"), 16)

    def spread(which, out):
        for slot, (odd_refs, even_refs, r) in enumerate(
            (
                ((ra_ref, corner_a_ref), (rb_ref, corner_b_ref), 1),
                ((rb_ref, corner_b_ref), (ra_ref, corner_a_ref), 0),
            )
        ):
            own, left, right = (
                jnp.where(ha_odd == 1, odd.astype(f32), even.astype(f32))
                for odd, even in (
                    (odd_refs[0][which, r], even_refs[0][which, r]),
                    *(
                        (odd_refs[1][side, which, r], even_refs[1][side, which, r])
                        for side in (1 - wa_odd, wa_odd)
                    ),
                )
            )
            at = 2 * which + slot
            gather_line(wide, wide_turned, at, own, left[1:2], right[:1], out, slot * cols)

    spread(0, x_ends)
    pre = [correlate_own(xs, x_ends, one_ref, cols, group) for group in range(2)]
    spread(1, g_ends)
    grad_active = [correlate_own(gs, g_ends, two_flip_ref, cols, group) for group in range(2)]

    active_t, slopes = [], []
    for group in range(2):
        value = pre[group]
        cdf = 0.5 * (1.0 + lax.erf(value * root_half))
        slopes.append(cdf + value * inv_root_two_pi * jnp.exp(-0.5 * value * value))
        active_t.append(transposed(value * cdf, turned_refs[group]))

    half, lead = CH // 2, 8
    low_half = lax.broadcasted_iota(jnp.int32, (CH, 2 * CH), 1) < CH
    low = low_half[:half]

    def kernel_grad_parts(fixed, acc_ref, a):
        parts = [[None] * 4 for _ in range(3)]

        def put(window, e, tile):
            old = parts[2 - window][e]
            parts[2 - window][e] = tile if old is None else old + tile

        for group in range(2):
            window = own_windows(gs, g_ends, group, cols, 1 - a)
            acc = acc_ref.at[group]
            acc[...] = jnp.dot(fixed[group], window, preferred_element_type=f32)
            for j in range(4):
                for t in range(8):
                    (window, i), (next_window, next_i) = divmod(2 * t, 5), divmod(2 * t + 1, 5)
                    e = j - i + 1 + group
                    c = j - next_i + 1 + group
                    joined = next_window in (window, 3)
                    use_left = 0 <= e < 4 if joined else 0 <= e < 3
                    use_right = not joined and 0 <= c < 3
                    if not (use_left or use_right):
                        continue
                    tile = acc[64 * j : 64 * j + 64, 128 * t : 128 * t + 128]
                    if use_left:
                        whole = joined or e == 0
                        put(window, e, tile if whole else jnp.where(low_half, tile, 0.0))
                    if use_right:
                        whole = c == 2
                        put(next_window, c + 1, tile if whole else jnp.where(low_half, 0.0, tile))
        return parts

    def put_tile(k, tap, left, right):
        sums[k, lead + half * tap : lead + half * tap + half, :] = jnp.where(low, left, right)

    def add_taps(a, parts):
        for b in range(3):
            for c in range(3):
                left, right = parts[b][c], parts[b][c + 1]
                put_tile(
                    1,
                    9 * a + 3 * b + c,
                    left[:half] + pltpu.roll(right[:half], CH, 1),
                    pltpu.roll(left[half:], CH, 1) + right[half:],
                )

    def first_grad(fixed, a):
        parts = [[None] * 4 for _ in range(3)]

        def put(window, e, tile):
            old = parts[window][e + 1]
            parts[window][e + 1] = tile if old is None else old + tile

        for group in range(2):
            window = own_windows(xs, x_ends, group, cols, a - 1)
            acc_ref = acc_one.at[2 * a + group]
            acc_ref[...] = jnp.dot(fixed[group], window, preferred_element_type=f32)
            for j in range(4):
                for t in range(8):
                    (window, i), (next_window, next_i) = divmod(2 * t, 5), divmod(2 * t + 1, 5)
                    e = i - j + 1 - group
                    c = next_i - j + 1 - group
                    joined = next_window in (window, 3)
                    use_left = -1 <= e < 3 if joined else 0 <= e < 3
                    use_right = not joined and 0 <= c < 3
                    if not (use_left or use_right):
                        continue
                    tile = acc_ref[64 * j : 64 * j + 64, 128 * t : 128 * t + 128]
                    if use_left:
                        whole = joined or e == 2
                        put(window, e, tile if whole else jnp.where(low_half, tile, 0.0))
                    if use_right:
                        whole = c == 0
                        put(next_window, c - 1, tile if whole else jnp.where(low_half, 0.0, tile))

        def joined_halves(b, c, d):
            first = parts[b][c + 1] + pltpu.roll(parts[b][c], CH, 1)
            second = pltpu.roll(parts[b][d + 1], CH, 1) + parts[b][d]
            return jnp.where(low_half, first, second)

        for b in range(3):
            for k, (c, d) in enumerate(((0, 1), (2, 2))):
                slot = swap.at[2 * (3 * a + b) + k]
                slot[:, :CH] = jnp.transpose(joined_halves(b, c, d))
                for tap, at in ((c, 0), (d, CH))[: 1 + (c != d)]:
                    even = slot[pl.ds(at, half, stride=2), :]
                    odd = slot[pl.ds(at + 1, half, stride=2), :]
                    put_tile(0, 9 * a + 3 * b + tap, even, pltpu.roll(odd, CH, 1))

    add_taps(0, kernel_grad_parts(active_t, acc_two.at[0], 0))
    grad_pre_t = []
    for group in range(2):
        grad_pre = grad_active[group] * slopes[group]
        grad_pre_ref[:, 256 * group : 256 * group + 256] = grad_pre.astype(bf16)
        grad_pre_t.append(jnp.transpose(grad_pre).astype(bf16))
    for a in range(3):
        first_grad(grad_pre_t, a)
    for a in (1, 2):
        add_taps(a, kernel_grad_parts(active_t, acc_two.at[a], a))

    if len(kg_refs) == 1:
        for k in range(2):
            kg_refs[0][k] = sums[k, lead : lead + 27 * half, :]
        return
    keep_ref, send_ref = kg_refs
    slabs, width, share, _ = keep_ref.shape
    take = 27 * half // (2 * slabs * width)
    full, left_over = take // 8 * 8, take % 8
    head = lax.broadcasted_iota(jnp.int32, (8, 2 * CH), 0) < left_over

    def chunk(d):
        at = lead + take * d + nothing
        first = sums[0, pl.ds(at, full + 8), :]
        second = sums[1, pl.ds(at - left_over, share - full), :]
        seam = jnp.where(head, first[full:], second[:8])
        return jnp.concatenate([first[:full], seam, second[8:]], axis=0)

    for z in range(slabs):
        for w in range(width):
            even, odd = (chunk((2 * z + c) * width + w) for c in range(2))
            keep_ref[z, w] = jnp.where(ha_odd == 0, even, odd)
            send_ref[z, w] = jnp.where(ha_odd == 0, odd, even).astype(bf16)


def ring_kernel(
    rows,
    cols,
    x_ref,
    g_ref,
    ra_ref,
    rb_ref,
    wa_ref,
    wb_ref,
    corner_a_ref,
    corner_b_ref,
    one_ref,
    two_flip_ref,
    grad_pre_ref,
    ps,
    *scratch,
):
    f32 = jnp.float32
    xs, gs, x_side, g_side = scratch[:4]
    select_ref = scratch[11]
    select_ref[...] = halo_selection(rows + 4, select_ref.shape)
    wide_refs, edges_ref = scratch[4:7], scratch[10]
    spread, gather_lines, put_wide, split_lanes = field_tools(
        rows,
        cols,
        ra_ref,
        rb_ref,
        wa_ref,
        wb_ref,
        corner_a_ref,
        corner_b_ref,
        select_ref,
        (wide_refs, scratch[7:10], edges_ref),
    )
    lines, stride, base = rows + 4, cols + PAD, 8
    side_rows = 2 * lines
    ha, wa = lax.axis_index("ha"), lax.axis_index("wa")
    ha_last = lax.axis_size("ha") - 1
    wa_last = lax.axis_size("wa") - 1
    runs = [(1, 1), (rows + 2, 1)]
    gathered = [(0, 3), (lines - 3, lines)]
    spread(0, x_ref, xs, x_side, gathered)
    pre = correlate(xs, x_side, one_ref, cols, runs)
    spread(1, g_ref, gs, g_side, gathered)
    grad_active = correlate(gs, g_side, two_flip_ref, cols, runs)
    position = lax.broadcasted_iota(jnp.int32, (side_rows, 256), 0)
    line = lax.rem(position, lines)
    dead = ((line < 2) & (ha == 0)) | ((line >= rows + 2) & (ha == ha_last))
    dead = dead | ((position < lines) & (wa == 0)) | ((position >= lines) & (wa == wa_last))
    wide, edges = wide_refs[2], edges_ref.at[2]
    for r in range(rows):
        own = grad_pre_ref[r * cols : r * cols + cols, :].astype(f32)
        put_wide(wide, base + PAD + (r + 2) * stride, cols, split_lanes(own))
    for group in range(2):
        value = pre[group]
        cdf = 0.5 * (1.0 + lax.erf(value * root_half))
        slope = cdf + value * inv_root_two_pi * jnp.exp(-0.5 * value * value)
        grad_pre = grad_active[group] * slope
        above = jnp.where(ha == 0, 0.0, grad_pre[:cols])
        below = jnp.where(ha == ha_last, 0.0, grad_pre[cols : 2 * cols])
        for l, part in ((1, above), (rows + 2, below)):
            start = base + PAD + l * stride
            put_wide(wide, start, cols, [part[:, :128], part[:, 128:]], 2 * group)
        edges[:side_rows, 256 * group : 256 * group + 256] = jnp.where(
            dead, 0.0, grad_pre[2 * cols :]
        )
    for l in range(1, rows + 3):
        left, right = base + l * stride + PAD - 1, base + (l + 1) * stride
        put_wide(wide, left, 1, split_lanes(edges[l : l + 1, :]))
        put_wide(wide, right, 1, split_lanes(edges[lines + l : lines + l + 1, :]))
    gather_lines(2, 1, rows + 3, ps)


def scratch_shapes(rows, cols, lanes, fields):
    span = (rows + 4) * (cols + PAD) + PAD
    wide = pltpu.VMEM((lanes // 128, span + 16, 128), jnp.float32)
    return [*[wide] * (2 * fields), pltpu.VMEM((fields, 6 * (rows + 4), lanes), jnp.float32)]


def main(shape, operands, split):
    rows, cols, lanes = shape
    if split:
        slabs, width = split
        take = 27 * CH // 2 // (2 * slabs * width)
        share = -(-2 * take // 8) * 8
        grads = tuple(
            jax.ShapeDtypeStruct((slabs, width, share, 2 * CH), dtype)
            for dtype in (jnp.float32, jnp.bfloat16)
        )
    else:
        grads = (jax.ShapeDtypeStruct((2, 27 * CH // 2, 2 * CH), jnp.float32),)
    vmem = pl.BlockSpec(memory_space=pltpu.VMEM)
    ends = pltpu.VMEM((2, 2 * cols, 1024), jnp.bfloat16)
    turning = pltpu.VMEM((rows * cols // 128, 256, 128), jnp.float32)
    return pl.pallas_call(
        functools.partial(main_kernel, cols),
        out_shape=(jax.ShapeDtypeStruct((rows * cols, lanes), jnp.bfloat16), *grads),
        in_specs=[vmem] * 8,
        out_specs=(vmem,) * (1 + len(grads)),
        scratch_shapes=[
            ends,
            ends,
            pltpu.VMEM((2, 27 * CH // 2 + 40, 2 * CH), jnp.float32),
            pltpu.VMEM((6, 256, 1024), jnp.float32),
            pltpu.VMEM((3, 2, 256, 1024), jnp.float32),
            turning,
            turning,
            pltpu.VMEM((18, 2 * CH, 2 * CH), jnp.float32),
            *line_scratch(4, cols, lanes),
        ],
        compiler_params=pltpu.CompilerParams(vmem_limit_bytes=32 << 20),
        cost_estimate=pl.CostEstimate(
            flops=10_000_000_000, bytes_accessed=8_000_000, transcendentals=1_000_000
        ),
    )(*operands)


def ring(fields, bands, grad_pre):
    rows, cols, lanes = fields[0].shape
    vmem = pl.BlockSpec(memory_space=pltpu.VMEM)
    moving = ((2, (rows + 4) * cols, 1024), jnp.bfloat16)
    lines = rows + 4
    side = pltpu.VMEM((2, 3, 2 * lines, 1024), jnp.bfloat16)
    return pl.pallas_call(
        functools.partial(ring_kernel, rows, cols),
        out_shape=jax.ShapeDtypeStruct(*moving),
        in_specs=[vmem] * 11,
        out_specs=vmem,
        scratch_shapes=[
            pltpu.VMEM(*moving),
            pltpu.VMEM(*moving),
            side,
            side,
            *scratch_shapes(rows, cols, lanes, 3),
            pltpu.VMEM(((lines + 1) * PAD + 18 * lines, 6 * lines), jnp.bfloat16),
        ],
        compiler_params=pltpu.CompilerParams(vmem_limit_bytes=20 << 20),
        cost_estimate=pl.CostEstimate(
            flops=3_000_000_000, bytes_accessed=8_000_000, transcendentals=500_000
        ),
    )(*fields, *bands, grad_pre)


def input_grad(ps, band, shape):
    rows, cols, _ = shape
    vmem = pl.BlockSpec(memory_space=pltpu.VMEM)
    return pl.pallas_call(
        functools.partial(input_grad_kernel, rows, cols),
        out_shape=jax.ShapeDtypeStruct(shape, jnp.bfloat16),
        in_specs=[vmem, vmem],
        out_specs=vmem,
        scratch_shapes=[pltpu.VMEM((9, 4, CH, 2 * CH), jnp.bfloat16)],
        compiler_params=pltpu.CompilerParams(vmem_limit_bytes=8 << 20),
        cost_estimate=pl.CostEstimate(
            flops=2_000_000_000, bytes_accessed=4_000_000, transcendentals=0
        ),
    )(ps, band)


def xor_exchange(block, axis, mask):
    count = lax.axis_size(axis)
    return lax.ppermute(block, axis, [(i, i ^ mask) for i in range(count)])


def total_of(refs):
    total = refs[0].astype(jnp.float32)
    for ref in refs[1:]:
        total = total + ref.astype(jnp.float32)
    return total


def sum_chip_kernel(keep_ref, got_ref, own_ref, *send_refs):
    wa = lax.axis_index("wa")
    for z in range(keep_ref.shape[0]):
        own_ref[z] = total_of([keep_ref[z, wa], got_ref[z, wa]])
        for k, ref in enumerate(send_refs, 1):
            ref[z] = total_of([keep_ref[z, wa ^ k], got_ref[z, wa ^ k]]).astype(ref.dtype)


def sum_wa_kernel(*refs):
    slabs = refs[0].shape[0]
    got_refs, (own_ref, *send_refs) = refs[:-slabs], refs[-slabs:]
    z = lax.div(lax.axis_index("ha"), 2)
    own_ref[...] = total_of([ref[z] for ref in got_refs])
    for k, ref in enumerate(send_refs, 1):
        ref[...] = total_of([got[z ^ k] for got in got_refs]).astype(ref.dtype)


def sum_z_kernel(*refs):
    total = total_of([ref[...] for ref in refs[:-2]])
    take = refs[-1].shape[0]
    for k, ref in enumerate(refs[-2:]):
        ref[...] = total[k * take : (k + 1) * take]


def reduce_chunks(keep, send, take):
    slabs, width = keep.shape[:2]
    f32, bf16 = jnp.float32, jnp.bfloat16
    unit = keep.shape[2:]
    got = xor_exchange(send, "ha", 1)
    shapes = [jax.ShapeDtypeStruct((slabs,) + unit, f32)]
    shapes += [jax.ShapeDtypeStruct((slabs,) + unit, bf16)] * (width - 1)
    own, *sends = small_call(sum_chip_kernel, tuple(shapes), keep, got)
    got = []
    for k, block in enumerate(sends, 1):
        got.append(xor_exchange(block, "wa", k))
    shapes = [jax.ShapeDtypeStruct(unit, f32)]
    shapes += [jax.ShapeDtypeStruct(unit, f32)] * (slabs - 1)
    own, *sends = small_call(sum_wa_kernel, tuple(shapes), own, *got)
    got = []
    for k, block in enumerate(sends, 1):
        got.append(xor_exchange(block, "ha", 2 * k))
    shapes = (jax.ShapeDtypeStruct((take, 2 * CH), f32),) * 2
    return small_call(sum_z_kernel, shapes, own, *got)


def shards(inputs, grad_out, kernel_one, kernel_two):
    height_count = lax.axis_size("ha")
    width_count = lax.axis_size("wa")
    devices = height_count * width_count
    x, g, to_a, to_b, own_a, own_b = pack(inputs, grad_out)
    wb = pair_exchange(own_b, "wa", 1)
    wa = pair_exchange(own_a, "wa", 0)
    ra = pair_exchange(to_a, "ha", 0)
    rb = pair_exchange(to_b, "ha", 1)
    one, two_flip, xs, gs = prepare(x, g, wa, wb, kernel_one, kernel_two)
    corner_to_a, corner_to_b = corners(wa, wb)
    corner_b = pair_exchange(corner_to_b, "ha", 1)
    corner_a = pair_exchange(corner_to_a, "ha", 0)

    split = None
    if (
        (27 * CH // 2) % devices == 0
        and height_count & (height_count - 1) == 0
        and width_count & (width_count - 1) == 0
        and height_count > 1
    ):
        split = (height_count // 2, width_count)
    fields = (x, g, ra, rb, wa, wb, corner_a, corner_b)
    bands = (one, two_flip)
    operands = (ra, rb, corner_a, corner_b, xs, gs, one, two_flip)
    grad_pre, *grads = main(inputs.shape, operands, split)
    ps = ring(fields, bands, grad_pre)
    grad_inputs = input_grad(ps, kernel_one, inputs.shape)
    if split:
        grads = reduce_chunks(*grads, 27 * CH // 2 // devices)
    else:
        grads = [
            lax.psum_scatter(
                grads[0][k].reshape(devices, -1), ("ha", "wa"), scatter_dimension=0, tiled=True
            )
            for k in range(2)
        ]
    return (grad_inputs, grads[0].reshape(-1), grads[1].reshape(-1))


def solution(mesh):
    return jax.shard_map(
        shards,
        mesh=mesh,
        in_specs=(P("ha", "wa", None), P("ha", "wa", None), P(), P()),
        out_specs=(P("ha", "wa", None), P(("ha", "wa")), P(("ha", "wa"))),
        check_vma=False,
    )
```
